512 devices in a mesh: slab: 64 (over z, x_lo, core), shell: 8 (over y, x_hi).
Axes of the slice: x: 4 (x_hi: 2, x_lo: 2; x = x_hi * 2 + x_lo), y: 4, z: 16, core: 2. Of those that a mesh axis runs over, the one named last changes fastest.
Arguments:
- images: bfloat16 [8192, 2, 16384], P('slab', None, 'shell'), may hold values from -6 to 6
- defocus: bfloat16 [8192], P('slab'), may hold values from 20 to 200
- pose_bin: int32 [8192, 1], P('slab'), may hold values from 0 to 63; in each aligned block of 128 rows (0 to 127, 128 to 255, ...) at most 6 rows name the same one
- freq_sq: float32 [16384], P('shell'), may hold values from 0 to 1, as said below
- model_slice: float32 [64, 2, 16384], P('slab', None, 'shell'), may hold values from -6 to 6
- interp_coef: bfloat16 [64, 128, 4, 128, 128], P('slab', 'shell'), may hold values from -0.5 to 0.5
- block_index: int32 [64, 128, 4], P('slab', 'shell'), may hold values from 0 to 2047, as said below
Outputs:
- volume_grad: float32 [2048, 2, 128], P(('slab', 'shell'))
The draws below stay inside these ranges and needn't reach their ends.
Inputs may be any that keep to these rules, and one draw needn't show every extreme that they name: `pose_bin`: among the images of one index of slab, no pose bin is named by more than 6 images, a bound that some block reaches. `freq_sq`: band s of the 8 bands of samples holds values between (s / 8) squared and ((s + 1) / 8) squared. `block_index`: among the 64 dense blocks of one pose bin in one shell band, the volume blocks v with the same v // 32 are named at most 2 times, and one such group exactly 2 times.
All inputs are finite; a program needn't handle non-finite values.
Results may differ from the reference program's by a relative error of at most 0.0029.
Values may be sent and summed in bfloat16 or wider, within the bound.
A program may use at most 64 MiB of HBM per device.

```python
import math
import jax
import jax.numpy as jnp
import numpy as np
from jax import lax

IMG_DEV = 128
NVB_DEV = 4
PIX = 16384
PB = 128
VB = 128
NNZ = 4
IMAGES = 8192
BINS = 64
BANDS = 8
CAP = 6
KB = 128
KBD = 16
TERMS = 64
CAPV = 2
NV = 2048
N_SLAB = 64


def draw_freq_sq(key, part):
    width = PIX // BANDS
    band = (jnp.arange(PIX, dtype=jnp.int32) // width).astype(jnp.float32)
    unit = jax.random.uniform(jax.random.fold_in(key, 11), (PIX,), jnp.float32)
    radius = (band + unit) / BANDS
    return jnp.clip(radius * radius, 0.0, 1.0)


def one_group(key):
    keys = jax.random.split(key, 4)
    group = NVB_DEV * BANDS
    first = jax.random.randint(keys[0], (), 0, N_SLAB)
    slots = jax.random.permutation(keys[1], (N_SLAB - 1) * CAPV)
    others = slots // CAPV
    others = others + (others >= first).astype(jnp.int32)
    owners = jnp.concatenate([jnp.full((CAPV,), first, jnp.int32), others[:TERMS - CAPV].astype(jnp.int32)])
    order = jax.random.permutation(keys[2], TERMS)
    owners = owners[order]
    local_block = jax.random.randint(keys[3], (TERMS,), 0, group)
    return (owners * group + local_block).astype(jnp.int32).reshape(KBD, NNZ)


def draw_block_index(key, part):
    base = jax.random.fold_in(key, 29)
    keys = jax.vmap(lambda n: jax.random.fold_in(base, n))(jnp.arange(BINS * BANDS, dtype=jnp.int32))
    blocks = jax.vmap(one_group)(keys)
    return blocks.reshape(BINS, KB, NNZ)


def steps_of(rng, shape, cuts, smallest, top_value):
    def one(dim, shards_of):
        heights = jax.random.uniform(jax.random.fold_in(jax.random.fold_in(rng, 6), dim), (shards_of,), jnp.float32, smallest / len(cuts), top_value / len(cuts))
        return jnp.repeat(jnp.exp(heights), shape[dim] // shards_of).reshape((-1,) + (1,) * (len(shape) - dim - 1))

    factor_of = one(*cuts[0])
    for cut in cuts[1:]:
        factor_of = factor_of * one(*cut)
    return factor_of


def shared_out(key, own, number, rows, number_of, top, limit, lean):
    order = jax.random.permutation(key, number_of)
    heavy_load, common = shares(number_of, rows * top, limit, lean, True), shares(number_of, rows * top, limit, lean, False)
    places = jnp.arange(number_of)

    def named(tallies, offset_by):
        used = int((tallies > 0).sum())
        fixed = max(1, used // 4)
        moved = fixed + (places - fixed + offset_by * (used - fixed)) % max(1, number_of - fixed)
        return jnp.zeros((number_of,), jnp.int32).at[order[jnp.where(places < fixed, places, moved)]].set(jnp.asarray(tallies, jnp.int32))

    tallies = jnp.where(number % 4 == 0, named(heavy_load, number // 4), named(common, number - number // 4 - 1))
    mixed = jax.random.permutation(jax.random.fold_in(own, 3), number_of)
    giver, receiver = mixed[0:number_of // 2 * 2:2], mixed[1:number_of // 2 * 2:2]
    room = jnp.minimum(tallies[giver] - 1, limit - tallies[receiver]) // 2
    room = jnp.where((giver == order[0]) | (receiver == order[0]) | (tallies[receiver] == 0), 0, jnp.maximum(room, 0))
    moved = jax.random.randint(jax.random.fold_in(own, 4), (number_of // 2,), 0, 1 << 20) % (room + 1)
    tallies = tallies.at[giver].add(-moved).at[receiver].add(moved)
    items = jnp.searchsorted(jnp.cumsum(tallies), jnp.arange(rows * top), side="right").astype(jnp.int32)
    table = items.reshape(top, rows).T
    table = table[jax.random.permutation(jax.random.fold_in(own, 1), rows)]
    offset_by = jax.random.randint(jax.random.fold_in(own, 2), (rows, 1), 0, top)
    return jnp.take_along_axis(table, (jnp.arange(top)[None, :] + offset_by) % top, axis=1)


def shares(amount, total, reach, skew, full):
    portions = [(1 << 20) // math.isqrt(standing ** skew) + 1 for standing in range(1, amount + 1)]
    largest = reach if full else min(reach, max(-(-total // amount), total * portions[0] // sum(portions)))
    least = 1 if total - largest >= amount - 1 else 0
    holding, surplus = [largest] + [least] * (amount - 1), total - largest - least * (amount - 1)
    while surplus > 0:
        candidates = [i for i in range(1, amount) if holding[i] < largest] or [i for i in range(1, amount) if holding[i] < reach]
        mass, left = sum([portions[i] for i in candidates]), surplus
        for i in candidates:
            addition = min(reach - holding[i], max(1, left * portions[i] // mass), surplus)
            holding[i] = holding[i] + addition
            surplus = surplus - addition
    return np.array(holding)


def centred(rng, dims, deviation, reach, cuts=(), kind=jnp.bfloat16):
    gain = steps_of(rng, dims, cuts, -0.22, 0.18) if cuts else 1.0
    values = jax.random.normal(rng, dims, jnp.float32) * deviation * gain
    return jnp.minimum(jnp.maximum(values, -reach), reach).astype(kind)


def setup_inputs(seed: int = 0) -> dict:
    seeds = jax.random.split(jax.random.key(seed), 8)
    images = centred(seeds[0], (IMAGES, 2, PIX), 1.0, 6.0, ((0, 64), (2, 8)))
    defocus = jnp.clip(jnp.exp(math.log(200.0) - 2.3025851 * jax.random.uniform(seeds[1], (IMAGES,), jnp.float32) ** steps_of(seeds[1], (IMAGES,), ((0, 64),), -0.2, 0.2)), 20.0, 200.0).astype(jnp.bfloat16)
    pose_bin_keys = jax.random.split(jax.random.fold_in(seeds[2], 1), IMAGES // IMG_DEV)
    pose_bin_turns = jax.random.permutation(jax.random.fold_in(seeds[2], 3), IMAGES // IMG_DEV)
    pose_bin = jax.vmap(lambda own, number: shared_out(jax.random.fold_in(seeds[2], 2), own, number, IMG_DEV, BINS, 1, CAP, 2))(pose_bin_keys, pose_bin_turns).reshape((IMAGES, 1))
    freq_sq = draw_freq_sq(jax.random.fold_in(seeds[7], 71), 0)
    model_slice = centred(seeds[4], (BINS, 2, PIX), 1.0, 6.0, ((0, 64), (2, 8)), jnp.float32)
    interp_coef = centred(seeds[5], (BINS, KB, NNZ, PB, VB), PB ** -0.5, 0.5, ((0, 64), (1, 8)))
    block_index = draw_block_index(jax.random.fold_in(seeds[7], 71), 0)
    return dict(images=images, defocus=defocus, pose_bin=pose_bin, freq_sq=freq_sq, model_slice=model_slice, interp_coef=interp_coef, block_index=block_index)


def reference(images, defocus, pose_bin, freq_sq, model_slice, interp_coef, block_index):
    f32 = jnp.float32
    bin_ids = jnp.arange(BINS, dtype=jnp.int32)

    def accumulate(carry, which):
        numerator, power = carry
        start = which.astype(jnp.int32) * IMG_DEV
        rows = lax.dynamic_slice_in_dim(images, start, IMG_DEV, 0).astype(f32)
        focus = lax.dynamic_slice_in_dim(defocus, start, IMG_DEV, 0).astype(f32)
        labels = lax.dynamic_slice_in_dim(pose_bin, start, IMG_DEV, 0)[:, 0]
        onehot = (labels[:, None] == bin_ids[None, :]).astype(f32)
        contrast = jnp.sin(focus[:, None] * freq_sq[None, :])
        numerator = numerator + jnp.einsum("ib,ics->bcs", onehot, contrast[:, None, :] * rows, precision=lax.Precision.HIGHEST)
        power = power + jnp.dot(onehot.T, contrast * contrast, precision=lax.Precision.HIGHEST)
        return (numerator, power), None

    start_carry = (jnp.zeros((BINS, 2, PIX), f32), jnp.zeros((BINS, PIX), f32))
    (numerator, power), _ = lax.scan(accumulate, start_carry, jnp.arange(N_SLAB, dtype=jnp.int32))
    residual_slice = ((power[:, None, :] * model_slice - numerator) / IMG_DEV).astype(jnp.bfloat16)

    def insert(grad, pieces):
        slice_one, coef_one, index_one = pieces
        tiles = slice_one.reshape(2, KB, PB).astype(f32)
        terms = jnp.einsum("ckp,kjpv->kjcv", tiles, coef_one.astype(f32), precision=lax.Precision.HIGHEST)
        grad = grad.at[index_one.reshape(-1)].add(terms.reshape(-1, 2, VB))
        return grad, None

    volume_grad, _ = lax.scan(insert, jnp.zeros((NV, 2, VB), f32), (residual_slice, interp_coef, block_index))
    return volume_grad
```

```python
import functools

import jax
import jax.numpy as jnp
from jax import lax
from jax.experimental import pallas as pl
from jax.experimental.pallas import tpu as pltpu
from jax.sharding import PartitionSpec as P

F32 = jnp.float32
BF16 = jnp.bfloat16
MESH = pl.DeviceIdType.MESH

QUAD = 4
SHELLS = 8
CAP = 6
LANES = 128
CHUNKS = 4
RUN = 4
PLANE = QUAD * SHELLS

INV_PI = 0.3183098861837907
PI_A, PI_B, PI_C = 3.140625, 9.67502593994140625e-4, 1.509957990978376e-7
S3, S5, S7, S9, S11 = -1 / 6, 1 / 120, -1 / 5040, 1 / 362880, -1 / 39916800


def folded(x):
    n = jnp.floor(x * INV_PI + 0.5)
    r = ((x - n * PI_A) - n * PI_B) - n * PI_C
    t = r * r
    return r * (1.0 + t * (S3 + t * (S5 + t * (S7 + t * (S9 + t * S11))))), n


def sine(x):
    s, n = folded(x)
    odd = n - 2.0 * jnp.floor(n * 0.5)
    return s * (1.0 - 2.0 * odd)


def dot(a, b):
    return jnp.dot(a, b, preferred_element_type=F32)


def halves(x):
    high = x.astype(BF16)
    return high, (x - high.astype(F32)).astype(BF16)


def iota(shape, dim):
    return lax.broadcasted_iota(jnp.int32, shape, dim)


def down(row):
    return jnp.broadcast_to(row, (LANES, LANES)).T


def kernel(
    depth,
    pose_ref,
    focus_ref,
    freq_ref,
    model_ref,
    index_ref,
    images_ref,
    coef_ref,
    out_ref,
    img,
    coef,
    focus_col,
    pair_hot,
    spread,
    part,
    core_got,
    x_got,
    table,
    table_core,
    table_x,
    stage,
    z_out,
    z_got,
    note_out,
    note_got,
    column,
    power,
    resid,
    place,
    target,
    terms,
    slot_out,
    slot_got,
    plane_out,
    plane_got,
    img_sem,
    coef_sem,
    core_sem,
    x_sem,
    z_sem,
    note_sem,
    slot_sem,
    plane_sem,
):
    slab = lax.axis_index("slab")
    shell = lax.axis_index("shell")
    z, quad = slab // QUAD, slab % QUAD
    x_lo, core = quad // 2, quad % 2
    core_peer = z * QUAD + x_lo * 2 + (1 - core)
    x_peer = z * QUAD + (1 - x_lo) * 2 + core
    mine = quad * SHELLS + shell

    def at(slab_id, shell_id):
        return {"slab": slab_id, "shell": shell_id}

    def z_peer(j):
        return lax.rem(z + j, depth)

    def plane_peer(m):
        return lax.rem(mine + m, PLANE)

    barrier = pltpu.get_barrier_semaphore()

    @pl.loop(1, depth)
    def _(j):
        pl.semaphore_signal(barrier, inc=1, device_id=at(z_peer(j) * QUAD + quad, shell), device_id_type=MESH)

    @pl.loop(1, PLANE)
    def _(m):
        g = plane_peer(m)
        pl.semaphore_signal(barrier, inc=1, device_id=at(z * QUAD + g // SHELLS, g % SHELLS), device_id_type=MESH)

    width = RUN * LANES
    loads = [
        pltpu.make_async_copy(
            images_ref.at[:, pl.ds(ch * width, width)], img.at[:, pl.ds(ch * width, width)], img_sem.at[ch]
        )
        for ch in range(CHUNKS)
    ]
    for load in loads:
        load.start()
    coef_load = pltpu.make_async_copy(coef_ref, coef, coef_sem)
    coef_load.start()

    pose = pose_ref[...].astype(F32)
    pose_col = down(pose)
    focus_col[...] = down(focus_ref[...].astype(F32))
    same = (pose_col == pose) & (iota((LANES, LANES), 1) < iota((LANES, LANES), 0))
    rank = jnp.sum(same.astype(F32), axis=1, keepdims=True)
    lane = iota((LANES, LANES), 1)
    wanted = 64 + quad * CAP + rank.astype(jnp.int32)
    spots = jnp.where(lane == wanted, focus_col[...], 0.0).astype(BF16)
    row = iota((64, LANES), 0)
    bins = row % depth * QUAD + (row // depth) % 2 * 2 + row // (2 * depth)
    hot = (bins == pose_ref[...]).astype(F32).astype(BF16)
    table[...] = dot(hot, spots)
    twice = (iota((LANES, 2 * LANES), 1) // 2 == iota((LANES, 2 * LANES), 0)).astype(F32).astype(BF16)
    pose_pair = dot(jnp.broadcast_to(pose, (8, LANES)).astype(BF16), twice)[0:1]
    wide = iota((LANES, 2 * LANES), 0)
    r64 = wide % 64
    bin64 = r64 % depth * QUAD + (r64 // depth) % 2 * 2 + r64 // (2 * depth)
    parity = iota((LANES, 2 * LANES), 1) % 2
    pair_hot[...] = (
        ((bin64.astype(F32) == pose_pair) & (parity == wide // 64)).astype(F32).astype(BF16)
    )

    index = index_ref[...]
    k_of = (iota((16, LANES), 1) % 16 == iota((16, LANES), 0)).astype(F32).astype(BF16)
    mask = (iota((NNZ_ROWS, LANES), 1) // 16 == iota((NNZ_ROWS, LANES), 0)).astype(F32)
    slab_row = jnp.sum(dot((index // 32).astype(F32).astype(BF16), k_of) * mask, axis=0, keepdims=True)
    low_row = jnp.sum(dot((index % 32).astype(F32).astype(BF16), k_of) * mask, axis=0, keepdims=True)
    live = iota((1, LANES), 1) < 64
    slab_row = jnp.where(live, slab_row, -1.0)
    slab_col = down(slab_row)
    before = (slab_col == slab_row) & (iota((LANES, LANES), 0) < iota((LANES, LANES), 1))
    slot_row = jnp.where(live, 2.0 * slab_row + jnp.sum(before.astype(F32), axis=0, keepdims=True), -1.0)
    hits = (iota((LANES, LANES), 0).astype(F32) == slot_row).astype(F32)
    place[...] = hits.astype(BF16)
    plane_block = slab_row.astype(jnp.int32) % QUAD * 32 + low_row.astype(jnp.int32) + 1
    target[...] = jnp.broadcast_to(
        jnp.sum(hits * plane_block.astype(F32), axis=1, keepdims=True), (LANES, LANES)
    )

    for ch in range(CHUNKS):
        loads[ch].wait()

        @pl.loop(0, RUN)
        def _(q):
            k = ch * RUN + q
            contrast = sine(focus_col[...] * freq_ref[pl.ds(k, 1), :])
            spread[pl.ds(0, LANES, stride=2), :] = contrast
            spread[pl.ds(1, LANES, stride=2), :] = contrast
            picture = img[:, pl.ds(pl.multiple_of(k * LANES, LANES), LANES)].astype(F32)
            high, low = halves(spread[...] * picture)
            sums = dot(pair_hot[...], high) + dot(pair_hot[...], low)
            first = pl.multiple_of(q * LANES, LANES)
            part[ch, :, pl.ds(first, LANES)] = sums[0:64]
            part[ch, :, pl.ds(pl.multiple_of(width + first, LANES), LANES)] = sums[64:128]

    pl.semaphore_wait(barrier, depth - 1 + PLANE - 1)

    half = 2 * depth
    other_rows = pl.multiple_of((1 - core) * half, half)
    my_rows = pl.multiple_of(core * half, half)
    other_x = pl.multiple_of(core * half + (1 - x_lo) * depth, depth)
    my_x = pl.multiple_of(core * half + x_lo * depth, depth)

    def send(src, dst, sems, i, device):
        return pltpu.make_async_remote_copy(
            src_ref=src,
            dst_ref=dst,
            send_sem=sems.at[0, i],
            recv_sem=sems.at[1, i],
            device_id=device,
            device_id_type=MESH,
        )

    to_core = at(core_peer, shell)
    to_x = at(x_peer, shell)
    core_sends = [send(table.at[pl.ds(other_rows, half)], table_core, core_sem, CHUNKS, to_core)]
    for ch in range(CHUNKS):
        core_sends.append(send(part.at[ch, pl.ds(other_rows, half)], core_got.at[ch], core_sem, ch, to_core))
    for copy in core_sends:
        copy.start()

    core_sends[0].wait()
    table[pl.ds(my_rows, half), :] += table_core[...]
    x_sends = [send(table.at[pl.ds(other_x, depth)], table_x, x_sem, CHUNKS, to_x)]
    x_sends[0].start()
    for ch in range(CHUNKS):
        core_sends[ch + 1].wait()
        part[ch, pl.ds(my_rows, half), :] += core_got[ch]
        copy = send(part.at[ch, pl.ds(other_x, depth)], x_got.at[ch], x_sem, ch, to_x)
        copy.start()
        x_sends.append(copy)

    def along_z(out, got, i, j):
        peer = z_peer(j)
        return pltpu.make_async_remote_copy(
            src_ref=out.at[peer],
            dst_ref=got.at[depth - j],
            send_sem=i[0],
            recv_sem=i[1],
            device_id=at(peer * QUAD + quad, shell),
            device_id_type=MESH,
        )

    def all_of(out, got, i):
        return pltpu.make_async_remote_copy(
            src_ref=out.at[pl.ds(0, depth - 1)],
            dst_ref=got.at[pl.ds(1, depth - 1)],
            send_sem=i[0],
            recv_sem=i[1],
            device_id=at(z_peer(1) * QUAD + quad, shell),
            device_id_type=MESH,
        )

    x_sends[0].wait()
    own_table = table[pl.ds(my_x, depth), :] + table_x[...]
    lanes8 = iota((8, LANES), 1)
    for i in range(depth):
        note_out[i] = jnp.where(
            lanes8 < 64, target[i * 8 : i * 8 + 8, :], jnp.broadcast_to(own_table[i : i + 1, :], (8, LANES))
        )
    note_got[0] = note_out[z]
    note_sems = (note_sem.at[0], note_sem.at[1])

    @pl.loop(1, depth)
    def _(j):
        along_z(note_out, note_got, note_sems, j).start()

    for ch in range(CHUNKS):
        x_sends[ch + 1].wait()
        total = part[ch, pl.ds(my_x, depth), :] + x_got[ch]
        for b in range(2 * RUN):
            stage[ch, :, b, :] = total[:, b * LANES : (b + 1) * LANES]
        z_out[ch] = stage[ch].astype(BF16)

        @pl.loop(1, depth)
        def _(j):
            along_z(z_out.at[ch], z_got.at[ch], (z_sem.at[0, ch], z_sem.at[1, ch]), j).start()

    all_of(note_out, note_got, note_sems).wait()
    values = note_got[:, 0, :]
    for i in range(QUAD * CAP):
        column[i] = jnp.broadcast_to(values[:, 64 + i : 65 + i], (depth, LANES))

    @pl.loop(0, CHUNKS * RUN)
    def _(k):
        freq = freq_ref[pl.ds(k, 1), :]
        total = jnp.zeros((depth, LANES), F32)
        for i in range(QUAD * CAP):
            s, _ = folded(column[i] * freq)
            total = total + s * s
        power[pl.ds(k, 1), :] = jnp.sum(total, axis=0, keepdims=True)

    tile = note_got[...].reshape(depth * 8, LANES)
    to_block = jnp.broadcast_to(tile[:, 0:1], (LANES, LANES)).T
    target[...] = to_block
    terms[...] = jnp.zeros_like(terms)
    coef_load.wait()

    for ch in range(CHUNKS):
        all_of(z_out.at[ch], z_got.at[ch], (z_sem.at[0, ch], z_sem.at[1, ch])).wait()
        numerator = stage[ch, z]
        for j in range(1, depth):
            numerator = numerator + z_got[ch, j].astype(F32)
        for c in range(2):
            for q in range(RUN):
                k = ch * RUN + q
                model = model_ref[c : c + 1, k * LANES : (k + 1) * LANES]
                resid[c * 16 + k : c * 16 + k + 1, :] = (
                    power[k : k + 1, :] * model - numerator[c * RUN + q : c * RUN + q + 1, :]
                ) * (1.0 / 128)
        for q in range(RUN):
            k = ch * RUN + q
            left = jnp.concatenate([resid[k : k + 1, :], resid[16 + k : 17 + k, :]], axis=0).astype(BF16)
            for j in range(NNZ):
                term = dot(left, coef[k, j])
                t = j * 16 + k
                terms[t : t + 1, 0:LANES] = term[0:1]
                terms[t : t + 1, LANES : 2 * LANES] = term[1:2]

    high, low = halves(terms[...])
    slots = dot(place[...], high) + dot(place[...], low)
    slot_out[...] = slots.reshape(depth, 8, 2 * LANES)
    slot_got[0] = slot_out[z]
    slot_sems = (slot_sem.at[0], slot_sem.at[1])

    @pl.loop(1, depth)
    def _(j):
        along_z(slot_out, slot_got, slot_sems, j).start()

    adds = (target[...] == (iota((LANES, LANES), 0) + 1).astype(F32)).astype(F32).astype(BF16)
    all_of(slot_out, slot_got, slot_sems).wait()
    high, low = halves(slot_got[...].reshape(depth * 8, 2 * LANES))
    dense = dot(adds, high) + dot(adds, low)
    plane_out[pl.ds(0, LANES, stride=2), :] = dense[:, 0:LANES]
    plane_out[pl.ds(1, LANES, stride=2), :] = dense[:, LANES : 2 * LANES]

    @pl.loop(1, PLANE)
    def _(m):
        g = plane_peer(m)
        pltpu.make_async_remote_copy(
            src_ref=plane_out.at[pl.ds(pl.multiple_of(g * 8, 8), 8)],
            dst_ref=plane_got.at[pl.ds(pl.multiple_of((PLANE - m) * 8, 8), 8)],
            send_sem=plane_sem.at[0],
            recv_sem=plane_sem.at[1],
            device_id=at(z * QUAD + g // SHELLS, g % SHELLS),
            device_id_type=MESH,
        ).start()

    total = plane_out[pl.ds(pl.multiple_of(mine * 8, 8), 8), :]
    rest = 8 * (PLANE - 1)
    pltpu.make_async_remote_copy(
        src_ref=plane_out.at[pl.ds(0, rest)],
        dst_ref=plane_got.at[pl.ds(8, rest)],
        send_sem=plane_sem.at[0],
        recv_sem=plane_sem.at[1],
        device_id=to_core,
        device_id_type=MESH,
    ).wait()
    for m in range(1, PLANE):
        total = total + plane_got[m * 8 : m * 8 + 8, :]
    out_ref[...] = total


NNZ = 4
NNZ_ROWS = NNZ


def shards(images, defocus, pose_bin, freq_sq, model_slice, interp_coef, block_index):
    depth = lax.axis_size("slab") // QUAD
    rows, _, width = images.shape
    run = RUN * LANES
    vmem = pl.BlockSpec(memory_space=pltpu.VMEM)
    hbm = pl.BlockSpec(memory_space=pl.ANY)
    dma = pltpu.SemaphoreType.DMA
    out = pl.pallas_call(
        functools.partial(kernel, depth),
        out_shape=jax.ShapeDtypeStruct((8, LANES), F32),
        in_specs=[vmem] * 5 + [hbm] * 2,
        out_specs=vmem,
        scratch_shapes=[
            pltpu.VMEM((2 * rows, width), BF16),
            pltpu.VMEM(interp_coef.shape[1:], BF16),
            pltpu.VMEM((LANES, LANES), F32),
            pltpu.VMEM((LANES, 2 * LANES), BF16),
            pltpu.VMEM((2 * LANES, LANES), F32),
            pltpu.VMEM((CHUNKS, QUAD * depth, 2 * run), F32),
            pltpu.VMEM((CHUNKS, 2 * depth, 2 * run), F32),
            pltpu.VMEM((CHUNKS, depth, 2 * run), F32),
            pltpu.VMEM((QUAD * depth, LANES), F32),
            pltpu.VMEM((2 * depth, LANES), F32),
            pltpu.VMEM((depth, LANES), F32),
            pltpu.VMEM((CHUNKS, depth, 2 * RUN, LANES), F32),
            pltpu.VMEM((CHUNKS, depth, 2 * RUN, LANES), BF16),
            pltpu.VMEM((CHUNKS, depth, 2 * RUN, LANES), BF16),
            pltpu.VMEM((depth, 8, LANES), F32),
            pltpu.VMEM((depth, 8, LANES), F32),
            pltpu.VMEM((QUAD * CAP, depth, LANES), F32),
            pltpu.VMEM((16, LANES), F32),
            pltpu.VMEM((32, LANES), F32),
            pltpu.VMEM((LANES, LANES), BF16),
            pltpu.VMEM((LANES, LANES), F32),
            pltpu.VMEM((LANES, 2 * LANES), F32),
            pltpu.VMEM((depth, 8, 2 * LANES), F32),
            pltpu.VMEM((depth, 8, 2 * LANES), F32),
            pltpu.VMEM((PLANE * 8, LANES), F32),
            pltpu.VMEM((PLANE * 8, LANES), F32),
            dma((CHUNKS,)),
            dma,
            dma((2, CHUNKS + 1)),
            dma((2, CHUNKS + 1)),
            dma((2, CHUNKS)),
            dma((2,)),
            dma((2,)),
            dma((2,)),
        ],
        compiler_params=pltpu.CompilerParams(collective_id=0, has_side_effects=True),
        name="cryo_grad",
    )(
        pose_bin.reshape(1, rows),
        defocus.reshape(1, rows),
        freq_sq.reshape(width // LANES, LANES),
        model_slice[0],
        jnp.transpose(block_index[0]),
        images.reshape(2 * rows, width),
        interp_coef[0],
    )
    return out.reshape(4, 2, LANES)


def solution(mesh):
    return jax.shard_map(
        shards,
        mesh=mesh,
        in_specs=(
            P("slab", None, "shell"),
            P("slab"),
            P("slab", None),
            P("shell"),
            P("slab", None, "shell"),
            P("slab", "shell", None, None, None),
            P("slab", "shell", None),
        ),
        out_specs=P(("slab", "shell"), None, None),
        check_vma=False,
    )
```

```python
import functools

import jax
import jax.numpy as jnp
from jax import lax
from jax.experimental import pallas as pl
from jax.experimental.pallas import tpu as pltpu
from jax.sharding import PartitionSpec as P

F32 = jnp.float32
BF16 = jnp.bfloat16
MESH = pl.DeviceIdType.MESH

QUAD = 4
SHELLS = 8
CAP = 6
LANES = 128
CHUNKS = 4
RUN = 4
NEAR = [(dx, dy, dh) for dx in range(2) for dy in range(4) for dh in range(2)]
NEAR = sorted(NEAR, key=lambda d: -(min(d[1], 4 - d[1]) + abs(2 * d[2] - d[0])))[:-1]
PLANE = 16

INV_PI = 0.3183098861837907
PI_A, PI_B, PI_C = 3.140625, 9.67502593994140625e-4, 1.509957990978376e-7
S3, S5, S7, S9, S11 = -1 / 6, 1 / 120, -1 / 5040, 1 / 362880, -1 / 39916800


def folded(x):
    n = jnp.floor(x * INV_PI + 0.5)
    r = ((x - n * PI_A) - n * PI_B) - n * PI_C
    t = r * r
    return r * (1.0 + t * (S3 + t * (S5 + t * (S7 + t * (S9 + t * S11))))), n


def sine(x):
    s, n = folded(x)
    odd = n - 2.0 * jnp.floor(n * 0.5)
    return s * (1.0 - 2.0 * odd)


def dot(a, b):
    return jnp.dot(a, b, preferred_element_type=F32)


def halves(x):
    high = x.astype(BF16)
    return high, (x - high.astype(F32)).astype(BF16)


def iota(shape, dim):
    return lax.broadcasted_iota(jnp.int32, shape, dim)


def down(row):
    return jnp.broadcast_to(row, (LANES, LANES)).T


def kernel(
    depth,
    pose_hbm,
    focus_hbm,
    freq_hbm,
    model_hbm,
    index_hbm,
    images_ref,
    coef_ref,
    out_ref,
    pose_ref,
    focus_ref,
    freq_ref,
    model_ref,
    index_ref,
    img,
    coef,
    focus_col,
    pair_hot,
    spread,
    part,
    core_got,
    x_got,
    table,
    table_core,
    table_x,
    stage,
    z_out,
    z_got,
    note_out,
    note_got,
    column,
    power,
    resid,
    place,
    target,
    target_got,
    adds,
    terms,
    slot_out,
    slot_got,
    plane_out,
    plane_got,
    small_sem,
    img_sem,
    coef_sem,
    core_sem,
    x_sem,
    z_sem,
    note_sem,
    slot_sem,
    plane_sem,
):
    slab = lax.axis_index("slab")
    shell = lax.axis_index("shell")
    z, quad = slab // QUAD, slab % QUAD
    x_lo, core = quad // 2, quad % 2
    core_peer = z * QUAD + x_lo * 2 + (1 - core)
    x_peer = z * QUAD + (1 - x_lo) * 2 + core
    y, x_hi = shell // 2, shell % 2

    def at(slab_id, shell_id):
        return {"slab": slab_id, "shell": shell_id}

    def z_peer(j):
        return lax.rem(z + j, depth)

    def plane_peer(offset):
        dx, dy, dh = offset
        return (x_lo + dx) % 2, (y + dy) % 4 * 2 + (x_hi + dh) % 2

    width = RUN * LANES
    rows_ref = images_ref.reshape(2 * images_ref.shape[0], images_ref.shape[2])
    loads = [
        pltpu.make_async_copy(
            rows_ref.at[:, pl.ds(ch * width, width)], img.at[:, pl.ds(ch * width, width)], img_sem.at[ch]
        )
        for ch in range(CHUNKS)
    ]
    smalls = [
        pltpu.make_async_copy(src, dst, small_sem.at[i])
        for i, (src, dst) in enumerate(
            (
                (pose_hbm, pose_ref),
                (focus_hbm, focus_ref),
                (freq_hbm, freq_ref),
                (index_hbm, index_ref),
                (model_hbm, model_ref),
            )
        )
    ]
    for load in smalls + loads:
        load.start()
    coef_load = pltpu.make_async_copy(coef_ref, coef, coef_sem)
    coef_load.start()

    barrier = pltpu.get_barrier_semaphore()

    far_first = sorted(range(1, depth), key=lambda j: -min(j, depth - j))
    for j in far_first:
        for side in (core, 1 - core):
            pl.semaphore_signal(
                barrier, inc=1, device_id=at(z_peer(j) * QUAD + x_lo * 2 + side, shell), device_id_type=MESH
            )

    for offset in NEAR:
        peer_x, peer_shell = plane_peer(offset)
        pl.semaphore_signal(
            barrier, inc=1, device_id=at(z * QUAD + peer_x * 2 + core, peer_shell), device_id_type=MESH
        )
    pl.semaphore_signal(barrier, inc=1, device_id=at(core_peer, shell), device_id_type=MESH)

    smalls[0].wait()
    smalls[1].wait()
    pose = pose_ref[...].astype(F32)
    pose_col = down(pose)
    focus_col[...] = down(focus_ref[...].astype(F32))
    twice = (iota((LANES, 2 * LANES), 1) // 2 == iota((LANES, 2 * LANES), 0)).astype(F32).astype(BF16)
    pose_pair = dot(jnp.broadcast_to(pose, (8, LANES)).astype(BF16), twice)[0:1]
    wide = iota((LANES, 2 * LANES), 0)
    r64 = wide % 64
    bin64 = r64 % depth * QUAD + (r64 // depth) % 2 * 2 + r64 // (2 * depth)
    parity = iota((LANES, 2 * LANES), 1) % 2
    pair_hot[...] = (
        ((bin64.astype(F32) == pose_pair) & (parity == wide // 64)).astype(F32).astype(BF16)
    )

    smalls[2].wait()
    for ch in range(CHUNKS):
        loads[ch].wait()

        @pl.loop(0, RUN)
        def _(q):
            k = ch * RUN + q
            contrast = sine(focus_col[...] * freq_ref[pl.ds(k, 1), :])
            spread[pl.ds(0, LANES, stride=2), :] = contrast
            spread[pl.ds(1, LANES, stride=2), :] = contrast
            picture = img[:, pl.ds(pl.multiple_of(k * LANES, LANES), LANES)].astype(F32)
            high, low = halves(spread[...] * picture)
            sums = dot(pair_hot[...], high) + dot(pair_hot[...], low)
            first = pl.multiple_of(q * LANES, LANES)
            part[ch, :, pl.ds(first, LANES)] = sums[0:64]
            part[ch, :, pl.ds(pl.multiple_of(width + first, LANES), LANES)] = sums[64:128]

    pl.semaphore_wait(barrier, 2 * (depth - 1) + len(NEAR) + 1)

    half = 2 * depth
    other_rows = pl.multiple_of((1 - core) * half, half)
    my_rows = pl.multiple_of(core * half, half)
    other_x = pl.multiple_of(core * half + (1 - x_lo) * depth, depth)
    my_x = pl.multiple_of(core * half + x_lo * depth, depth)

    def send(src, dst, sems, i, device):
        return pltpu.make_async_remote_copy(
            src_ref=src,
            dst_ref=dst,
            send_sem=sems.at[0, i],
            recv_sem=sems.at[1, i],
            device_id=device,
            device_id_type=MESH,
        )

    to_core = at(core_peer, shell)
    to_x = at(x_peer, shell)
    core_sends = [
        send(part.at[ch, pl.ds(other_rows, half)], core_got.at[ch], core_sem, ch, to_core) for ch in range(CHUNKS)
    ]
    for copy in core_sends:
        copy.start()

    same = (pose_col == pose) & (iota((LANES, LANES), 1) < iota((LANES, LANES), 0))
    rank = jnp.sum(same.astype(F32), axis=1, keepdims=True)
    lane = iota((LANES, LANES), 1)
    wanted = 64 + quad * CAP + rank.astype(jnp.int32)
    spots = jnp.where(lane == wanted, focus_col[...], 0.0).astype(BF16)
    row = iota((64, LANES), 0)
    bins = row % depth * QUAD + (row // depth) % 2 * 2 + row // (2 * depth)
    hot = (bins == pose_ref[...]).astype(F32).astype(BF16)
    table[...] = dot(hot, spots)
    smalls[3].wait()
    index = index_ref[...]
    k_of = (iota((16, LANES), 1) % 16 == iota((16, LANES), 0)).astype(F32).astype(BF16)
    mask = (iota((NNZ_ROWS, LANES), 1) // 16 == iota((NNZ_ROWS, LANES), 0)).astype(F32)
    slab_row = jnp.sum(dot((index // 32).astype(F32).astype(BF16), k_of) * mask, axis=0, keepdims=True)
    low_row = jnp.sum(dot((index % 32).astype(F32).astype(BF16), k_of) * mask, axis=0, keepdims=True)
    live = iota((1, LANES), 1) < 64
    slab_row = jnp.where(live, slab_row, -1.0)
    slab_col = down(slab_row)
    before = (slab_col == slab_row) & (iota((LANES, LANES), 0) < iota((LANES, LANES), 1))
    rank_row = jnp.sum(before.astype(F32), axis=0, keepdims=True).astype(jnp.int32)
    slab_int = slab_row.astype(jnp.int32)
    x_of = slab_int % QUAD // 2
    slot_row = jnp.where(live, slab_int % 2 * 64 + slab_int // QUAD * 4 + x_of * 2 + rank_row, -1)
    place[...] = (iota((LANES, LANES), 0) == slot_row).astype(F32).astype(BF16)
    block_row = (x_of * 32 + low_row.astype(jnp.int32) + 1).astype(F32)
    at_z = ((slot_row // 4 == iota((2 * depth, LANES), 0)) & live).astype(F32).astype(BF16)
    at_lane = jnp.where(slot_row % 4 == iota((LANES, LANES), 0), block_row, 0.0).astype(BF16)
    target[...] = lax.dot_general(at_z, at_lane, (((1,), (1,)), ((), ())), preferred_element_type=F32)

    other_targets = pl.multiple_of((1 - core) * depth, depth)
    my_targets = pl.multiple_of(core * depth, depth)
    table_send = send(table.at[pl.ds(other_rows, half)], table_core, core_sem, CHUNKS, to_core)
    target_send = send(target.at[pl.ds(other_targets, depth)], target_got, core_sem, CHUNKS + 1, to_core)
    table_send.start()
    target_send.start()

    x_sends = []
    for ch in range(CHUNKS):
        core_sends[ch].wait()
        part[ch, pl.ds(my_rows, half), :] += core_got[ch]
        copy = send(part.at[ch, pl.ds(other_x, depth)], x_got.at[ch], x_sem, ch, to_x)
        copy.start()
        x_sends.append(copy)
        if ch == 0:
            table_send.wait()
            table[pl.ds(my_rows, half), :] += table_core[...]
            table_x_send = send(table.at[pl.ds(other_x, depth)], table_x, x_sem, CHUNKS, to_x)
            table_x_send.start()

    def along_z(out, got, i, j):
        peer = z_peer(j)
        return pltpu.make_async_remote_copy(
            src_ref=out.at[peer],
            dst_ref=got.at[depth - j],
            send_sem=i[0],
            recv_sem=i[1],
            device_id=at(peer * QUAD + quad, shell),
            device_id_type=MESH,
        )

    def all_of(out, got, i):
        return pltpu.make_async_remote_copy(
            src_ref=out.at[pl.ds(0, depth - 1)],
            dst_ref=got.at[pl.ds(1, depth - 1)],
            send_sem=i[0],
            recv_sem=i[1],
            device_id=at(z_peer(1) * QUAD + quad, shell),
            device_id_type=MESH,
        )

    note_sems = (note_sem.at[0], note_sem.at[1])
    for ch in range(CHUNKS):
        x_sends[ch].wait()
        total = part[ch, pl.ds(my_x, depth), :] + x_got[ch]
        for b in range(2 * RUN):
            stage[ch, :, b, :] = total[:, b * LANES : (b + 1) * LANES]
        z_out[ch] = stage[ch].astype(BF16)

        for j in far_first:
            along_z(z_out.at[ch], z_got.at[ch], (z_sem.at[0, ch], z_sem.at[1, ch]), j).start()
        if ch == 0:
            table_x_send.wait()
            target_send.wait()
            own_table = table[pl.ds(my_x, depth), :] + table_x[...]
            note_out[:, 0, :] = own_table + target[pl.ds(my_targets, depth), :] + pltpu.roll(target_got[...], 4, 1)
            note_got[0] = note_out[z]

            for j in far_first:
                along_z(note_out, note_got, note_sems, j).start()

    all_of(note_out, note_got, note_sems).wait()
    values = note_got[:, 0, :]
    for i in range(QUAD * CAP):
        column[i] = jnp.broadcast_to(values[:, 64 + i : 65 + i], (depth, LANES))

    @pl.loop(0, CHUNKS * RUN)
    def _(k):
        freq = freq_ref[pl.ds(k, 1), :]
        total = jnp.zeros((depth, LANES), F32)
        for i in range(QUAD * CAP):
            s, _ = folded(column[i] * freq)
            total = total + s * s
        power[pl.ds(k, 1), :] = jnp.sum(total, axis=0, keepdims=True)

    across = iota((LANES, LANES), 1)
    slot_of = (across // 64 * 4 + across % 4 == iota((LANES, LANES), 0)).astype(F32).astype(BF16)
    from_z = (iota((depth, LANES), 1) % 64 // 4 == iota((depth, LANES), 0)).astype(F32)
    to_block = jnp.sum(dot(values.astype(BF16), slot_of) * from_z, axis=0, keepdims=True)
    adds[...] = (to_block == (iota((64, LANES), 0) + 1).astype(F32)).astype(F32).astype(BF16)
    terms[...] = jnp.zeros_like(terms)
    coef_load.wait()
    smalls[4].wait()

    for ch in range(CHUNKS):
        all_of(z_out.at[ch], z_got.at[ch], (z_sem.at[0, ch], z_sem.at[1, ch])).wait()
        numerator = stage[ch, z]
        for j in range(1, depth):
            numerator = numerator + z_got[ch, j].astype(F32)
        for c in range(2):
            for q in range(RUN):
                k = ch * RUN + q
                model = model_ref[c : c + 1, k * LANES : (k + 1) * LANES]
                resid[c * 16 + k : c * 16 + k + 1, :] = (
                    power[k : k + 1, :] * model - numerator[c * RUN + q : c * RUN + q + 1, :]
                ) * (1.0 / 128)
        for q in range(RUN):
            k = ch * RUN + q
            left = jnp.concatenate([resid[k : k + 1, :], resid[16 + k : 17 + k, :]], axis=0).astype(BF16)
            for j in range(NNZ):
                term = dot(left, coef[k, j])
                t = j * 16 + k
                terms[t : t + 1, 0:LANES] = term[0:1]
                terms[t : t + 1, LANES : 2 * LANES] = term[1:2]

    high, low = halves(terms[...])
    slots = dot(place[...], high) + dot(place[...], low)
    slot_out[pl.ds(0, LANES, stride=2), :] = slots[:, 0:LANES]
    slot_out[pl.ds(1, LANES, stride=2), :] = slots[:, LANES : 2 * LANES]
    for j in far_first + [0]:
        for other in range(2):
            if j or other:
                side = 1 - core if other else core
                peer = z_peer(j)
                send(
                    slot_out.at[pl.ds(pl.multiple_of((side * depth + peer) * 8, 8), 8)],
                    slot_got.at[pl.ds((other * depth + (depth - j) % depth) * 8, 8)],
                    slot_sem,
                    0,
                    at(peer * QUAD + x_lo * 2 + side, shell),
                ).start()
    slot_got[0:8, :] = slot_out[pl.ds(pl.multiple_of((core * depth + z) * 8, 8), 8), :]
    rest = 8 * (2 * depth - 1)
    send(slot_out.at[pl.ds(0, rest)], slot_got.at[pl.ds(8, rest)], slot_sem, 0, to_core).wait()
    for c in range(2):
        high, low = halves(slot_got[pl.ds(c, LANES, stride=2), :])
        plane_out[pl.ds(c, 64, stride=2), :] = dot(adds[...], high) + dot(adds[...], low)

    for offset in NEAR:
        peer_x, peer_shell = plane_peer(offset)
        spot = NEAR.index((offset[0], -offset[1] % 4, offset[2]))
        send(
            plane_out.at[pl.ds(pl.multiple_of((peer_x * SHELLS + peer_shell) * 8, 8), 8)],
            plane_got.at[pl.ds(spot * 8, 8)],
            plane_sem,
            0,
            at(z * QUAD + peer_x * 2 + core, peer_shell),
        ).start()
    total = plane_out[pl.ds(pl.multiple_of((x_lo * SHELLS + shell) * 8, 8), 8), :]
    rest = 8 * len(NEAR)
    send(plane_out.at[pl.ds(0, rest)], plane_got, plane_sem, 0, to_core).wait()
    for i in range(len(NEAR)):
        total = total + plane_got[i * 8 : i * 8 + 8, :]
    out_ref[...] = total


NNZ = 4
NNZ_ROWS = NNZ


def shards(images, defocus, pose_bin, freq_sq, model_slice, interp_coef, block_index):
    depth = lax.axis_size("slab") // QUAD
    rows, _, width = images.shape
    run = RUN * LANES
    vmem = pl.BlockSpec(memory_space=pltpu.VMEM)
    hbm = pl.BlockSpec(memory_space=pl.ANY)
    dma = pltpu.SemaphoreType.DMA
    out = pl.pallas_call(
        functools.partial(kernel, depth),
        out_shape=jax.ShapeDtypeStruct((8, LANES), F32),
        in_specs=[hbm] * 7,
        out_specs=vmem,
        scratch_shapes=[
            pltpu.VMEM((1, rows), jnp.int32),
            pltpu.VMEM((1, rows), BF16),
            pltpu.VMEM((width // LANES, LANES), F32),
            pltpu.VMEM((2, width), F32),
            pltpu.VMEM((NNZ, 16), jnp.int32),
            pltpu.VMEM((2 * rows, width), BF16),
            pltpu.VMEM(interp_coef.shape[1:], BF16),
            pltpu.VMEM((LANES, LANES), F32),
            pltpu.VMEM((LANES, 2 * LANES), BF16),
            pltpu.VMEM((2 * LANES, LANES), F32),
            pltpu.VMEM((CHUNKS, QUAD * depth, 2 * run), F32),
            pltpu.VMEM((CHUNKS, 2 * depth, 2 * run), F32),
            pltpu.VMEM((CHUNKS, depth, 2 * run), F32),
            pltpu.VMEM((QUAD * depth, LANES), F32),
            pltpu.VMEM((2 * depth, LANES), F32),
            pltpu.VMEM((depth, LANES), F32),
            pltpu.VMEM((CHUNKS, depth, 2 * RUN, LANES), F32),
            pltpu.VMEM((CHUNKS, depth, 2 * RUN, LANES), BF16),
            pltpu.VMEM((CHUNKS, depth, 2 * RUN, LANES), BF16),
            pltpu.VMEM((depth, 1, LANES), F32),
            pltpu.VMEM((depth, 1, LANES), F32),
            pltpu.VMEM((QUAD * CAP, depth, LANES), F32),
            pltpu.VMEM((16, LANES), F32),
            pltpu.VMEM((32, LANES), F32),
            pltpu.VMEM((LANES, LANES), BF16),
            pltpu.VMEM((2 * depth, LANES), F32),
            pltpu.VMEM((depth, LANES), F32),
            pltpu.VMEM((64, LANES), BF16),
            pltpu.VMEM((LANES, 2 * LANES), F32),
            pltpu.VMEM((2 * LANES, LANES), F32),
            pltpu.VMEM((2 * LANES, LANES), F32),
            pltpu.VMEM((PLANE * 8, LANES), F32),
            pltpu.VMEM((len(NEAR) * 8, LANES), F32),
            dma((5,)),
            dma((CHUNKS,)),
            dma,
            dma((2, CHUNKS + 2)),
            dma((2, CHUNKS + 1)),
            dma((2, CHUNKS)),
            dma((2,)),
            dma((2, 1)),
            dma((2, 1)),
        ],
        compiler_params=pltpu.CompilerParams(collective_id=0, has_side_effects=True),
        name="cryo_grad",
    )(
        pose_bin.reshape(1, rows),
        defocus.reshape(1, rows),
        freq_sq.reshape(width // LANES, LANES),
        model_slice[0],
        jnp.transpose(block_index[0]),
        images,
        interp_coef[0],
    )
    return out.reshape(4, 2, LANES)


def solution(mesh):
    return jax.shard_map(
        shards,
        mesh=mesh,
        in_specs=(
            P("slab", None, "shell"),
            P("slab"),
            P("slab", None),
            P("shell"),
            P("slab", None, "shell"),
            P("slab", "shell", None, None, None),
            P("slab", "shell", None),
        ),
        out_specs=P(("slab", "shell"), None, None),
        check_vma=False,
    )
```

```python
import functools

import jax
import jax.numpy as jnp
from jax import lax
from jax.experimental import pallas as pl
from jax.experimental.pallas import tpu as pltpu
from jax.sharding import PartitionSpec as P

F32 = jnp.float32
BF16 = jnp.bfloat16
MESH = pl.DeviceIdType.MESH

QUAD = 4
SHELLS = 8
CAP = 6
LANES = 128
CHUNKS = 4
RUN = 4
NEAR = [(dx, dy, dh) for dx in range(2) for dy in range(4) for dh in range(2)]
NEAR = sorted(NEAR, key=lambda d: -(min(d[1], 4 - d[1]) + abs(2 * d[2] - d[0])))[:-1]
PLANE = 16

INV_PI = 0.3183098861837907
PI_A, PI_B, PI_C = 3.140625, 9.67502593994140625e-4, 1.509957990978376e-7
S3, S5, S7, S9, S11 = -1 / 6, 1 / 120, -1 / 5040, 1 / 362880, -1 / 39916800


def folded(x):
    n = jnp.floor(x * INV_PI + 0.5)
    r = ((x - n * PI_A) - n * PI_B) - n * PI_C
    t = r * r
    return r * (1.0 + t * (S3 + t * (S5 + t * (S7 + t * (S9 + t * S11))))), n


def sine(x):
    s, n = folded(x)
    odd = n - 2.0 * jnp.floor(n * 0.5)
    return s * (1.0 - 2.0 * odd)


def dot(a, b):
    return jnp.dot(a, b, preferred_element_type=F32)


def halves(x):
    high = x.astype(BF16)
    return high, (x - high.astype(F32)).astype(BF16)


def iota(shape, dim):
    return lax.broadcasted_iota(jnp.int32, shape, dim)


def down(row):
    return jnp.broadcast_to(row, (LANES, LANES)).T


def kernel(
    depth,
    pose_hbm,
    focus_hbm,
    freq_hbm,
    model_hbm,
    index_hbm,
    images_ref,
    coef_ref,
    out_ref,
    pose_ref,
    focus_ref,
    freq_ref,
    model_ref,
    index_ref,
    img,
    coef,
    focus_col,
    pair_hot,
    spread,
    part,
    core_got,
    x_got,
    table,
    table_core,
    table_x,
    stage,
    z_out,
    z_got,
    note_out,
    note_got,
    column,
    power,
    resid,
    place,
    target,
    target_got,
    adds,
    terms,
    slot_out,
    slot_got,
    plane_out,
    plane_got,
    far_sem,
    small_sem,
    img_sem,
    coef_sem,
    core_sem,
    x_sem,
    z_sem,
    note_sem,
    slot_sem,
    plane_sem,
):
    slab = lax.axis_index("slab")
    shell = lax.axis_index("shell")
    z, quad = slab // QUAD, slab % QUAD
    x_lo, core = quad // 2, quad % 2
    core_peer = z * QUAD + x_lo * 2 + (1 - core)
    x_peer = z * QUAD + (1 - x_lo) * 2 + core
    y, x_hi = shell // 2, shell % 2

    def at(slab_id, shell_id):
        return {"slab": slab_id, "shell": shell_id}

    def z_peer(j):
        return lax.rem(z + j, depth)

    def plane_peer(offset):
        dx, dy, dh = offset
        return (x_lo + dx) % 2, (y + dy) % 4 * 2 + (x_hi + dh) % 2

    width = RUN * LANES
    rows_ref = images_ref.reshape(2 * images_ref.shape[0], images_ref.shape[2])
    loads = [
        pltpu.make_async_copy(
            rows_ref.at[:, pl.ds(ch * width, width)], img.at[:, pl.ds(ch * width, width)], img_sem.at[ch]
        )
        for ch in range(CHUNKS)
    ]
    smalls = [
        pltpu.make_async_copy(src, dst, small_sem.at[i])
        for i, (src, dst) in enumerate(
            (
                (pose_hbm, pose_ref),
                (focus_hbm, focus_ref),
                (freq_hbm, freq_ref),
                (index_hbm, index_ref),
                (model_hbm, model_ref),
            )
        )
    ]
    for load in smalls + loads:
        load.start()
    coef_load = pltpu.make_async_copy(coef_ref, coef, coef_sem)
    coef_load.start()

    barrier = pltpu.get_barrier_semaphore()

    far_first = sorted(range(1, depth), key=lambda j: -min(j, depth - j))
    reach = depth // 4
    close = [j for j in far_first if min(j, depth - j) <= reach]
    for j in close:
        pl.semaphore_signal(barrier, inc=1, device_id=at(z_peer(j) * QUAD + quad, shell), device_id_type=MESH)

    for offset in NEAR:
        peer_x, peer_shell = plane_peer(offset)
        pl.semaphore_signal(
            barrier, inc=1, device_id=at(z * QUAD + peer_x * 2 + core, peer_shell), device_id_type=MESH
        )
    pl.semaphore_signal(barrier, inc=1, device_id=at(core_peer, shell), device_id_type=MESH)

    smalls[0].wait()
    smalls[1].wait()
    pose = pose_ref[...].astype(F32)
    pose_col = down(pose)
    focus_col[...] = down(focus_ref[...].astype(F32))
    twice = (iota((LANES, 2 * LANES), 1) // 2 == iota((LANES, 2 * LANES), 0)).astype(F32).astype(BF16)
    pose_pair = dot(jnp.broadcast_to(pose, (8, LANES)).astype(BF16), twice)[0:1]
    wide = iota((LANES, 2 * LANES), 0)
    r64 = wide % 64
    bin64 = r64 % depth * QUAD + (r64 // depth) % 2 * 2 + r64 // (2 * depth)
    parity = iota((LANES, 2 * LANES), 1) % 2
    pair_hot[...] = (
        ((bin64.astype(F32) == pose_pair) & (parity == wide // 64)).astype(F32).astype(BF16)
    )

    half = 2 * depth
    other_rows = pl.multiple_of((1 - core) * half, half)
    my_rows = pl.multiple_of(core * half, half)
    other_x = pl.multiple_of(core * half + (1 - x_lo) * depth, depth)
    my_x = pl.multiple_of(core * half + x_lo * depth, depth)

    def send(src, dst, sems, i, device):
        return pltpu.make_async_remote_copy(
            src_ref=src,
            dst_ref=dst,
            send_sem=sems.at[0, i],
            recv_sem=sems.at[1, i],
            device_id=device,
            device_id_type=MESH,
        )

    to_core = at(core_peer, shell)
    to_x = at(x_peer, shell)
    def summed(ch):
        loads[ch].wait()

        @pl.loop(0, RUN)
        def _(q):
            k = ch * RUN + q
            contrast = sine(focus_col[...] * freq_ref[pl.ds(k, 1), :])
            spread[pl.ds(0, LANES, stride=2), :] = contrast
            spread[pl.ds(1, LANES, stride=2), :] = contrast
            picture = img[:, pl.ds(pl.multiple_of(k * LANES, LANES), LANES)].astype(F32)
            high, low = halves(spread[...] * picture)
            sums = dot(pair_hot[...], high) + dot(pair_hot[...], low)
            first = pl.multiple_of(q * LANES, LANES)
            part[ch, :, pl.ds(first, LANES)] = sums[0:64]
            part[ch, :, pl.ds(pl.multiple_of(width + first, LANES), LANES)] = sums[64:128]

    core_sends = [
        send(part.at[ch, pl.ds(other_rows, half)], core_got.at[ch], core_sem, ch, to_core) for ch in range(CHUNKS)
    ]
    x_sends = [
        send(part.at[ch, pl.ds(other_x, depth)], x_got.at[ch], x_sem, ch, to_x) for ch in range(CHUNKS)
    ]

    def pass_on(ch):
        core_sends[ch].wait()
        part[ch, pl.ds(my_rows, half), :] += core_got[ch]
        x_sends[ch].start()

    smalls[2].wait()
    summed(0)
    pl.semaphore_wait(barrier, len(close) + len(NEAR) + 1)
    core_sends[0].start()
    for j in (reach, depth - reach):
        pl.semaphore_signal(far_sem, inc=1, device_id=at(z_peer(j) * QUAD + quad, shell), device_id_type=MESH)

    same = (pose_col == pose) & (iota((LANES, LANES), 1) < iota((LANES, LANES), 0))
    rank = jnp.sum(same.astype(F32), axis=1, keepdims=True)
    lane = iota((LANES, LANES), 1)
    wanted = 64 + quad * CAP + rank.astype(jnp.int32)
    spots = jnp.where(lane == wanted, focus_col[...], 0.0).astype(BF16)
    row = iota((64, LANES), 0)
    bins = row % depth * QUAD + (row // depth) % 2 * 2 + row // (2 * depth)
    hot = (bins == pose_ref[...]).astype(F32).astype(BF16)
    table[...] = dot(hot, spots)
    smalls[3].wait()
    index = index_ref[...]
    k_of = (iota((16, LANES), 1) % 16 == iota((16, LANES), 0)).astype(F32).astype(BF16)
    mask = (iota((NNZ_ROWS, LANES), 1) // 16 == iota((NNZ_ROWS, LANES), 0)).astype(F32)
    slab_row = jnp.sum(dot((index // 32).astype(F32).astype(BF16), k_of) * mask, axis=0, keepdims=True)
    low_row = jnp.sum(dot((index % 32).astype(F32).astype(BF16), k_of) * mask, axis=0, keepdims=True)
    live = iota((1, LANES), 1) < 64
    slab_row = jnp.where(live, slab_row, -1.0)
    slab_col = down(slab_row)
    before = (slab_col == slab_row) & (iota((LANES, LANES), 0) < iota((LANES, LANES), 1))
    rank_row = jnp.sum(before.astype(F32), axis=0, keepdims=True).astype(jnp.int32)
    slab_int = slab_row.astype(jnp.int32)
    x_of = slab_int % QUAD // 2
    slot_row = jnp.where(live, slab_int % 2 * 64 + slab_int // QUAD * 4 + x_of * 2 + rank_row, -1)
    place[...] = (iota((LANES, LANES), 0) == slot_row).astype(F32).astype(BF16)
    block_row = (x_of * 32 + low_row.astype(jnp.int32) + 1).astype(F32)
    at_z = ((slot_row // 4 == iota((2 * depth, LANES), 0)) & live).astype(F32).astype(BF16)
    at_lane = jnp.where(slot_row % 4 == iota((LANES, LANES), 0), block_row, 0.0).astype(BF16)
    target[...] = lax.dot_general(at_z, at_lane, (((1,), (1,)), ((), ())), preferred_element_type=F32)

    other_targets = pl.multiple_of((1 - core) * depth, depth)
    my_targets = pl.multiple_of(core * depth, depth)
    table_send = send(table.at[pl.ds(other_rows, half)], table_core, core_sem, CHUNKS, to_core)
    target_send = send(target.at[pl.ds(other_targets, depth)], target_got, core_sem, CHUNKS + 1, to_core)
    table_send.start()
    target_send.start()

    table_x_send = send(table.at[pl.ds(other_x, depth)], table_x, x_sem, CHUNKS, to_x)
    for ch in range(1, CHUNKS):
        summed(ch)
        core_sends[ch].start()
        if ch == 2:
            pass_on(0)
            table_send.wait()
            table[pl.ds(my_rows, half), :] += table_core[...]
            table_x_send.start()
    for ch in range(1, CHUNKS):
        pass_on(ch)

    def along_z(out, got, i, j):
        peer = z_peer(j)
        return pltpu.make_async_remote_copy(
            src_ref=out.at[peer],
            dst_ref=got.at[depth - j],
            send_sem=i[0],
            recv_sem=i[1],
            device_id=at(peer * QUAD + quad, shell),
            device_id_type=MESH,
        )

    def all_of(out, got, i):
        return pltpu.make_async_remote_copy(
            src_ref=out.at[pl.ds(0, depth - 1)],
            dst_ref=got.at[pl.ds(1, depth - 1)],
            send_sem=i[0],
            recv_sem=i[1],
            device_id=at(z_peer(1) * QUAD + quad, shell),
            device_id_type=MESH,
        )

    note_sems = (note_sem.at[0], note_sem.at[1])
    pl.semaphore_wait(far_sem, 2)
    for ch in range(CHUNKS):
        x_sends[ch].wait()
        total = part[ch, pl.ds(my_x, depth), :] + x_got[ch]
        for b in range(2 * RUN):
            stage[ch, :, b, :] = total[:, b * LANES : (b + 1) * LANES]
        z_out[ch] = stage[ch].astype(BF16)

        for j in far_first:
            along_z(z_out.at[ch], z_got.at[ch], (z_sem.at[0, ch], z_sem.at[1, ch]), j).start()
        if ch == 0:
            table_x_send.wait()
            target_send.wait()
            own_table = table[pl.ds(my_x, depth), :] + table_x[...]
            note_out[:, 0, :] = own_table + target[pl.ds(my_targets, depth), :] + pltpu.roll(target_got[...], 4, 1)
            note_got[0] = note_out[z]

            for j in far_first:
                along_z(note_out, note_got, note_sems, j).start()

    all_of(note_out, note_got, note_sems).wait()
    values = note_got[:, 0, :]
    for i in range(QUAD * CAP):
        column[i] = jnp.broadcast_to(values[:, 64 + i : 65 + i], (depth, LANES))

    @pl.loop(0, CHUNKS * RUN)
    def _(k):
        freq = freq_ref[pl.ds(k, 1), :]
        total = jnp.zeros((depth, LANES), F32)
        for i in range(QUAD * CAP):
            s, _ = folded(column[i] * freq)
            total = total + s * s
        power[pl.ds(k, 1), :] = jnp.sum(total, axis=0, keepdims=True)

    across = iota((LANES, LANES), 1)
    slot_of = (across // 64 * 4 + across % 4 == iota((LANES, LANES), 0)).astype(F32).astype(BF16)
    from_z = (iota((depth, LANES), 1) % 64 // 4 == iota((depth, LANES), 0)).astype(F32)
    to_block = jnp.sum(dot(values.astype(BF16), slot_of) * from_z, axis=0, keepdims=True)
    adds[...] = (to_block == (iota((64, LANES), 0) + 1).astype(F32)).astype(F32).astype(BF16)
    terms[...] = jnp.zeros_like(terms)
    coef_load.wait()
    smalls[4].wait()

    for ch in range(CHUNKS):
        all_of(z_out.at[ch], z_got.at[ch], (z_sem.at[0, ch], z_sem.at[1, ch])).wait()
        numerator = stage[ch, z]
        for j in range(1, depth):
            numerator = numerator + z_got[ch, j].astype(F32)
        for c in range(2):
            for q in range(RUN):
                k = ch * RUN + q
                model = model_ref[c : c + 1, k * LANES : (k + 1) * LANES]
                resid[c * 16 + k : c * 16 + k + 1, :] = (
                    power[k : k + 1, :] * model - numerator[c * RUN + q : c * RUN + q + 1, :]
                ) * (1.0 / 128)
        for q in range(RUN):
            k = ch * RUN + q
            left = jnp.concatenate([resid[k : k + 1, :], resid[16 + k : 17 + k, :]], axis=0).astype(BF16)
            for j in range(NNZ):
                term = dot(left, coef[k, j])
                t = j * 16 + k
                terms[t : t + 1, 0:LANES] = term[0:1]
                terms[t : t + 1, LANES : 2 * LANES] = term[1:2]

    high, low = halves(terms[...])
    slots = dot(place[...], high) + dot(place[...], low)
    slot_out[pl.ds(0, LANES, stride=2), :] = slots[:, 0:LANES]
    slot_out[pl.ds(1, LANES, stride=2), :] = slots[:, LANES : 2 * LANES]
    for j in far_first + [0]:
        for other in range(2):
            if j or other:
                side = 1 - core if other else core
                peer = z_peer(j)
                send(
                    slot_out.at[pl.ds(pl.multiple_of((side * depth + peer) * 8, 8), 8)],
                    slot_got.at[pl.ds((other * depth + (depth - j) % depth) * 8, 8)],
                    slot_sem,
                    0,
                    at(peer * QUAD + x_lo * 2 + side, shell),
                ).start()
    slot_got[0:8, :] = slot_out[pl.ds(pl.multiple_of((core * depth + z) * 8, 8), 8), :]
    rest = 8 * (2 * depth - 1)
    send(slot_out.at[pl.ds(0, rest)], slot_got.at[pl.ds(8, rest)], slot_sem, 0, to_core).wait()
    for c in range(2):
        high, low = halves(slot_got[pl.ds(c, LANES, stride=2), :])
        plane_out[pl.ds(c, 64, stride=2), :] = dot(adds[...], high) + dot(adds[...], low)

    for offset in NEAR:
        peer_x, peer_shell = plane_peer(offset)
        spot = NEAR.index((offset[0], -offset[1] % 4, offset[2]))
        send(
            plane_out.at[pl.ds(pl.multiple_of((peer_x * SHELLS + peer_shell) * 8, 8), 8)],
            plane_got.at[pl.ds(spot * 8, 8)],
            plane_sem,
            0,
            at(z * QUAD + peer_x * 2 + core, peer_shell),
        ).start()
    total = plane_out[pl.ds(pl.multiple_of((x_lo * SHELLS + shell) * 8, 8), 8), :]
    rest = 8 * len(NEAR)
    send(plane_out.at[pl.ds(0, rest)], plane_got, plane_sem, 0, to_core).wait()
    for i in range(len(NEAR)):
        total = total + plane_got[i * 8 : i * 8 + 8, :]
    out_ref[...] = total


NNZ = 4
NNZ_ROWS = NNZ


def shards(images, defocus, pose_bin, freq_sq, model_slice, interp_coef, block_index):
    depth = lax.axis_size("slab") // QUAD
    rows, _, width = images.shape
    run = RUN * LANES
    vmem = pl.BlockSpec(memory_space=pltpu.VMEM)
    hbm = pl.BlockSpec(memory_space=pl.ANY)
    dma = pltpu.SemaphoreType.DMA
    out = pl.pallas_call(
        functools.partial(kernel, depth),
        out_shape=jax.ShapeDtypeStruct((8, LANES), F32),
        in_specs=[hbm] * 7,
        out_specs=vmem,
        scratch_shapes=[
            pltpu.VMEM((1, rows), jnp.int32),
            pltpu.VMEM((1, rows), BF16),
            pltpu.VMEM((width // LANES, LANES), F32),
            pltpu.VMEM((2, width), F32),
            pltpu.VMEM((NNZ, 16), jnp.int32),
            pltpu.VMEM((2 * rows, width), BF16),
            pltpu.VMEM(interp_coef.shape[1:], BF16),
            pltpu.VMEM((LANES, LANES), F32),
            pltpu.VMEM((LANES, 2 * LANES), BF16),
            pltpu.VMEM((2 * LANES, LANES), F32),
            pltpu.VMEM((CHUNKS, QUAD * depth, 2 * run), F32),
            pltpu.VMEM((CHUNKS, 2 * depth, 2 * run), F32),
            pltpu.VMEM((CHUNKS, depth, 2 * run), F32),
            pltpu.VMEM((QUAD * depth, LANES), F32),
            pltpu.VMEM((2 * depth, LANES), F32),
            pltpu.VMEM((depth, LANES), F32),
            pltpu.VMEM((CHUNKS, depth, 2 * RUN, LANES), F32),
            pltpu.VMEM((CHUNKS, depth, 2 * RUN, LANES), BF16),
            pltpu.VMEM((CHUNKS, depth, 2 * RUN, LANES), BF16),
            pltpu.VMEM((depth, 1, LANES), F32),
            pltpu.VMEM((depth, 1, LANES), F32),
            pltpu.VMEM((QUAD * CAP, depth, LANES), F32),
            pltpu.VMEM((16, LANES), F32),
            pltpu.VMEM((32, LANES), F32),
            pltpu.VMEM((LANES, LANES), BF16),
            pltpu.VMEM((2 * depth, LANES), F32),
            pltpu.VMEM((depth, LANES), F32),
            pltpu.VMEM((64, LANES), BF16),
            pltpu.VMEM((LANES, 2 * LANES), F32),
            pltpu.VMEM((2 * LANES, LANES), F32),
            pltpu.VMEM((2 * LANES, LANES), F32),
            pltpu.VMEM((PLANE * 8, LANES), F32),
            pltpu.VMEM((len(NEAR) * 8, LANES), F32),
            pltpu.SemaphoreType.REGULAR,
            dma((5,)),
            dma((CHUNKS,)),
            dma,
            dma((2, CHUNKS + 2)),
            dma((2, CHUNKS + 1)),
            dma((2, CHUNKS)),
            dma((2,)),
            dma((2, 1)),
            dma((2, 1)),
        ],
        compiler_params=pltpu.CompilerParams(collective_id=0, has_side_effects=True, vmem_limit_bytes=20 << 20),
        name="cryo_grad",
    )(*(pltpu.with_memory_space_constraint(a, pltpu.HBM) for a in (
        pose_bin.reshape(1, rows),
        defocus.reshape(1, rows),
        freq_sq.reshape(width // LANES, LANES),
        model_slice[0],
        jnp.transpose(block_index[0]),
        images,
        interp_coef[0],
    )))
    return out.reshape(4, 2, LANES)


def solution(mesh):
    return jax.shard_map(
        shards,
        mesh=mesh,
        in_specs=(
            P("slab", None, "shell"),
            P("slab"),
            P("slab", None),
            P("shell"),
            P("slab", None, "shell"),
            P("slab", "shell", None, None, None),
            P("slab", "shell", None),
        ),
        out_specs=P(("slab", "shell"), None, None),
        check_vma=False,
    )
```

```python
import functools

import jax
import jax.numpy as jnp
from jax import lax
from jax.experimental import pallas as pl
from jax.experimental.pallas import tpu as pltpu
from jax.sharding import PartitionSpec as P

F32 = jnp.float32
BF16 = jnp.bfloat16
MESH = pl.DeviceIdType.MESH

QUAD = 4
SHELLS = 8
CAP = 6
LANES = 128
RUNS = (4, 4, 4, 4)
STARTS = tuple(sum(RUNS[:i]) for i in range(len(RUNS)))
CHUNKS = len(RUNS)
EARLY = (4, 12, 3, 13, 2, 14, 1, 15)
NEAR = [(dx, dy, dh) for dx in range(2) for dy in range(4) for dh in range(2)]
NEAR = sorted(NEAR, key=lambda d: -(min(d[1], 4 - d[1]) + abs(2 * d[2] - d[0])))[:-1]
PLANE = 16

INV_PI = 0.3183098861837907
PI_A, PI_B, PI_C = 3.140625, 9.67502593994140625e-4, 1.509957990978376e-7
S3, S5, S7, S9, S11 = -1 / 6, 1 / 120, -1 / 5040, 1 / 362880, -1 / 39916800


def folded(x):
    n = jnp.floor(x * INV_PI + 0.5)
    r = ((x - n * PI_A) - n * PI_B) - n * PI_C
    t = r * r
    return r * (1.0 + t * (S3 + t * (S5 + t * (S7 + t * (S9 + t * S11))))), n


def sine(x):
    s, n = folded(x)
    odd = n - 2.0 * jnp.floor(n * 0.5)
    return s * (1.0 - 2.0 * odd)


def dot(a, b):
    return jnp.dot(a, b, preferred_element_type=F32)


def halves(x):
    high = x.astype(BF16)
    return high, (x - high.astype(F32)).astype(BF16)


def iota(shape, dim):
    return lax.broadcasted_iota(jnp.int32, shape, dim)


def down(row):
    return jnp.broadcast_to(row, (LANES, LANES)).T


def kernel(
    depth,
    pose_hbm,
    focus_hbm,
    freq_hbm,
    model_hbm,
    index_hbm,
    images_ref,
    coef_ref,
    out_ref,
    pose_ref,
    focus_ref,
    freq_ref,
    model_ref,
    index_ref,
    img,
    coef,
    focus_col,
    pair_hot,
    spread,
    part,
    core_got,
    x_got,
    table,
    table_core,
    table_x,
    stage,
    z_out,
    z_got,
    note_out,
    note_got,
    column,
    power,
    resid,
    place,
    target,
    target_got,
    adds,
    terms,
    slot_out,
    slot_got,
    plane_out,
    plane_got,
    far_sem,
    small_sem,
    img_sem,
    coef_sem,
    core_sem,
    x_sem,
    z_sem,
    note_sem,
    slot_sem,
    plane_sem,
):
    slab = lax.axis_index("slab")
    shell = lax.axis_index("shell")
    z, quad = slab // QUAD, slab % QUAD
    x_lo, core = quad // 2, quad % 2
    core_peer = z * QUAD + x_lo * 2 + (1 - core)
    x_peer = z * QUAD + (1 - x_lo) * 2 + core
    y, x_hi = shell // 2, shell % 2

    def at(slab_id, shell_id):
        return {"slab": slab_id, "shell": shell_id}

    def z_peer(j):
        return lax.rem(z + j, depth)

    def plane_peer(offset):
        dx, dy, dh = offset
        return (x_lo + dx) % 2, (y + dy) % 4 * 2 + (x_hi + dh) % 2

    rows_ref = images_ref.reshape(2 * images_ref.shape[0], images_ref.shape[2])
    loads = [
        pltpu.make_async_copy(
            rows_ref.at[:, pl.ds(start * LANES, run * LANES)],
            img.at[:, pl.ds(start * LANES, run * LANES)],
            img_sem.at[ch],
        )
        for ch, (start, run) in enumerate(zip(STARTS, RUNS))
    ]
    smalls = [
        pltpu.make_async_copy(src, dst, small_sem.at[i])
        for i, (src, dst) in enumerate(
            (
                (pose_hbm, pose_ref),
                (focus_hbm, focus_ref),
                (freq_hbm, freq_ref),
                (index_hbm, index_ref),
                (model_hbm, model_ref),
            )
        )
    ]
    for load in smalls + loads:
        load.start()
    coef_load = pltpu.make_async_copy(coef_ref, coef, coef_sem)
    coef_load.start()

    barrier = pltpu.get_barrier_semaphore()

    far_first = sorted(range(1, depth), key=lambda j: -min(j, depth - j))
    reach = depth // 4
    close = [j for j in far_first if min(j, depth - j) <= reach]
    for j in close:
        pl.semaphore_signal(barrier, inc=1, device_id=at(z_peer(j) * QUAD + quad, shell), device_id_type=MESH)

    for offset in NEAR:
        peer_x, peer_shell = plane_peer(offset)
        pl.semaphore_signal(
            barrier, inc=1, device_id=at(z * QUAD + peer_x * 2 + core, peer_shell), device_id_type=MESH
        )
    pl.semaphore_signal(barrier, inc=1, device_id=at(core_peer, shell), device_id_type=MESH)

    smalls[0].wait()
    smalls[1].wait()
    pose = pose_ref[...].astype(F32)
    pose_col = down(pose)
    focus_col[...] = down(focus_ref[...].astype(F32))
    twice = (iota((LANES, 2 * LANES), 1) // 2 == iota((LANES, 2 * LANES), 0)).astype(F32).astype(BF16)
    pose_pair = dot(jnp.broadcast_to(pose, (8, LANES)).astype(BF16), twice)[0:1]
    wide = iota((LANES, 2 * LANES), 0)
    r64 = wide % 64
    bin64 = r64 % depth * QUAD + (r64 // depth) % 2 * 2 + r64 // (2 * depth)
    parity = iota((LANES, 2 * LANES), 1) % 2
    pair_hot[...] = (
        ((bin64.astype(F32) == pose_pair) & (parity == wide // 64)).astype(F32).astype(BF16)
    )

    half = 2 * depth
    other_rows = pl.multiple_of((1 - core) * half, half)
    my_rows = pl.multiple_of(core * half, half)
    other_x = pl.multiple_of(core * half + (1 - x_lo) * depth, depth)
    my_x = pl.multiple_of(core * half + x_lo * depth, depth)

    def send(src, dst, sems, i, device):
        return pltpu.make_async_remote_copy(
            src_ref=src,
            dst_ref=dst,
            send_sem=sems.at[0, i],
            recv_sem=sems.at[1, i],
            device_id=device,
            device_id_type=MESH,
        )

    to_core = at(core_peer, shell)
    to_x = at(x_peer, shell)
    def summed(ch):
        loads[ch].wait()

        @pl.loop(0, RUNS[ch])
        def _(q):
            k = STARTS[ch] + q
            contrast = sine(focus_col[...] * freq_ref[pl.ds(k, 1), :])
            spread[pl.ds(0, LANES, stride=2), :] = contrast
            spread[pl.ds(1, LANES, stride=2), :] = contrast
            picture = img[:, pl.ds(pl.multiple_of(k * LANES, LANES), LANES)].astype(F32)
            high, low = halves(spread[...] * picture)
            sums = dot(pair_hot[...], high) + dot(pair_hot[...], low)
            first = pl.multiple_of(q * LANES, LANES)
            second = pl.multiple_of(RUNS[ch] * LANES + first, LANES)
            part[ch][:, pl.ds(first, LANES)] = sums[0:64]
            part[ch][:, pl.ds(second, LANES)] = sums[64:128]

    core_sends = [
        send(part[ch].at[pl.ds(other_rows, half)], core_got[ch], core_sem, ch, to_core) for ch in range(CHUNKS)
    ]
    x_sends = [
        send(part[ch].at[pl.ds(other_x, depth)], x_got[ch], x_sem, ch, to_x) for ch in range(CHUNKS)
    ]

    def pass_on(ch):
        core_sends[ch].wait()
        part[ch][pl.ds(my_rows, half), :] += core_got[ch][...]
        x_sends[ch].start()

    smalls[2].wait()
    summed(0)
    pl.semaphore_wait(barrier, len(close) + len(NEAR) + 1)
    core_sends[0].start()
    for j in (reach, depth - reach):
        pl.semaphore_signal(far_sem, inc=1, device_id=at(z_peer(j) * QUAD + quad, shell), device_id_type=MESH)

    same = (pose_col == pose) & (iota((LANES, LANES), 1) < iota((LANES, LANES), 0))
    rank = jnp.sum(same.astype(F32), axis=1, keepdims=True)
    lane = iota((LANES, LANES), 1)
    wanted = 64 + quad * CAP + rank.astype(jnp.int32)
    spots = jnp.where(lane == wanted, focus_col[...], 0.0).astype(BF16)
    row = iota((64, LANES), 0)
    bins = row % depth * QUAD + (row // depth) % 2 * 2 + row // (2 * depth)
    hot = (bins == pose_ref[...]).astype(F32).astype(BF16)
    table[...] = dot(hot, spots)
    smalls[3].wait()
    index = index_ref[...]
    k_of = (iota((16, LANES), 1) % 16 == iota((16, LANES), 0)).astype(F32).astype(BF16)
    mask = (iota((NNZ_ROWS, LANES), 1) // 16 == iota((NNZ_ROWS, LANES), 0)).astype(F32)
    slab_row = jnp.sum(dot((index // 32).astype(F32).astype(BF16), k_of) * mask, axis=0, keepdims=True)
    low_row = jnp.sum(dot((index % 32).astype(F32).astype(BF16), k_of) * mask, axis=0, keepdims=True)
    live = iota((1, LANES), 1) < 64
    slab_row = jnp.where(live, slab_row, -1.0)
    slab_col = down(slab_row)
    before = (slab_col == slab_row) & (iota((LANES, LANES), 0) < iota((LANES, LANES), 1))
    rank_row = jnp.sum(before.astype(F32), axis=0, keepdims=True).astype(jnp.int32)
    slab_int = slab_row.astype(jnp.int32)
    x_of = slab_int % QUAD // 2
    slot_row = jnp.where(live, slab_int % 2 * 64 + slab_int // QUAD * 4 + x_of * 2 + rank_row, -1)
    place[...] = (iota((LANES, LANES), 0) == slot_row).astype(F32).astype(BF16)
    block_row = (x_of * 32 + low_row.astype(jnp.int32) + 1).astype(F32)
    at_z = ((slot_row // 4 == iota((2 * depth, LANES), 0)) & live).astype(F32).astype(BF16)
    at_lane = jnp.where(slot_row % 4 == iota((LANES, LANES), 0), block_row, 0.0).astype(BF16)
    target[...] = lax.dot_general(at_z, at_lane, (((1,), (1,)), ((), ())), preferred_element_type=F32)

    other_targets = pl.multiple_of((1 - core) * depth, depth)
    my_targets = pl.multiple_of(core * depth, depth)
    table_send = send(table.at[pl.ds(other_rows, half)], table_core, core_sem, CHUNKS, to_core)
    target_send = send(target.at[pl.ds(other_targets, depth)], target_got, core_sem, CHUNKS + 1, to_core)
    table_send.start()
    target_send.start()

    table_x_send = send(table.at[pl.ds(other_x, depth)], table_x, x_sem, CHUNKS, to_x)
    for ch in range(1, CHUNKS):
        summed(ch)
        core_sends[ch].start()
        if ch == 1:
            pass_on(0)
            table_send.wait()
            table[pl.ds(my_rows, half), :] += table_core[...]
            table_x_send.start()
    for ch in range(1, CHUNKS):
        pass_on(ch)

    def along_z(out, got, i, j):
        peer = z_peer(j)
        return pltpu.make_async_remote_copy(
            src_ref=out.at[peer],
            dst_ref=got.at[depth - j],
            send_sem=i[0],
            recv_sem=i[1],
            device_id=at(peer * QUAD + quad, shell),
            device_id_type=MESH,
        )

    def all_of(out, got, i):
        return pltpu.make_async_remote_copy(
            src_ref=out.at[pl.ds(0, depth - 1)],
            dst_ref=got.at[pl.ds(1, depth - 1)],
            send_sem=i[0],
            recv_sem=i[1],
            device_id=at(z_peer(1) * QUAD + quad, shell),
            device_id_type=MESH,
        )

    note_sems = (note_sem.at[0], note_sem.at[1])

    def z_send(ch, to):
        for j in to:
            along_z(z_out[ch], z_got[ch], (z_sem.at[0, ch], z_sem.at[1, ch]), j).start()

    for ch in range(CHUNKS):
        x_sends[ch].wait()
        total = part[ch][pl.ds(my_x, depth), :] + x_got[ch][...]
        for b in range(2 * RUNS[ch]):
            stage[ch][:, b, :] = total[:, b * LANES : (b + 1) * LANES]
        z_out[ch][...] = stage[ch][...].astype(BF16)
        if ch > 0:
            z_send(ch, far_first)
            continue
        z_send(0, EARLY)
        pl.semaphore_wait(far_sem, 2)
        z_send(0, [j for j in far_first if j not in EARLY])
        table_x_send.wait()
        target_send.wait()
        own_table = table[pl.ds(my_x, depth), :] + table_x[...]
        note_out[:, 0, :] = own_table + target[pl.ds(my_targets, depth), :] + pltpu.roll(target_got[...], 4, 1)
        note_got[0] = note_out[z]

        for j in far_first:
            along_z(note_out, note_got, note_sems, j).start()
    all_of(note_out, note_got, note_sems).wait()
    values = note_got[:, 0, :]
    for i in range(QUAD * CAP):
        column[i] = jnp.broadcast_to(values[:, 64 + i : 65 + i], (depth, LANES))

    @pl.loop(0, sum(RUNS))
    def _(k):
        freq = freq_ref[pl.ds(k, 1), :]
        total = jnp.zeros((depth, LANES), F32)
        for i in range(QUAD * CAP):
            s, _ = folded(column[i] * freq)
            total = total + s * s
        power[pl.ds(k, 1), :] = jnp.sum(total, axis=0, keepdims=True)

    across = iota((LANES, LANES), 1)
    slot_of = (across // 64 * 4 + across % 4 == iota((LANES, LANES), 0)).astype(F32).astype(BF16)
    from_z = (iota((depth, LANES), 1) % 64 // 4 == iota((depth, LANES), 0)).astype(F32)
    to_block = jnp.sum(dot(values.astype(BF16), slot_of) * from_z, axis=0, keepdims=True)
    adds[...] = (to_block == (iota((64, LANES), 0) + 1).astype(F32)).astype(F32).astype(BF16)
    terms[...] = jnp.zeros_like(terms)
    coef_load.wait()
    smalls[4].wait()

    for ch in range(CHUNKS):
        all_of(z_out[ch], z_got[ch], (z_sem.at[0, ch], z_sem.at[1, ch])).wait()
        numerator = stage[ch][z]
        for j in range(1, depth):
            numerator = numerator + z_got[ch][j].astype(F32)
        for c in range(2):
            for q in range(RUNS[ch]):
                k = STARTS[ch] + q
                model = model_ref[c : c + 1, k * LANES : (k + 1) * LANES]
                resid[c * 16 + k : c * 16 + k + 1, :] = (
                    power[k : k + 1, :] * model - numerator[c * RUNS[ch] + q : c * RUNS[ch] + q + 1, :]
                ) * (1.0 / 128)
        for q in range(RUNS[ch]):
            k = STARTS[ch] + q
            left = jnp.concatenate([resid[k : k + 1, :], resid[16 + k : 17 + k, :]], axis=0).astype(BF16)
            for j in range(NNZ):
                term = dot(left, coef[k, j])
                t = j * 16 + k
                terms[t : t + 1, 0:LANES] = term[0:1]
                terms[t : t + 1, LANES : 2 * LANES] = term[1:2]

    high, low = halves(terms[...])
    slots = dot(place[...], high) + dot(place[...], low)
    slot_out[pl.ds(0, LANES, stride=2), :] = slots[:, 0:LANES]
    slot_out[pl.ds(1, LANES, stride=2), :] = slots[:, LANES : 2 * LANES]
    for j in far_first + [0]:
        for other in range(2):
            if j or other:
                side = 1 - core if other else core
                peer = z_peer(j)
                send(
                    slot_out.at[pl.ds(pl.multiple_of((side * depth + peer) * 8, 8), 8)],
                    slot_got.at[pl.ds((other * depth + (depth - j) % depth) * 8, 8)],
                    slot_sem,
                    0,
                    at(peer * QUAD + x_lo * 2 + side, shell),
                ).start()
    slot_got[0:8, :] = slot_out[pl.ds(pl.multiple_of((core * depth + z) * 8, 8), 8), :]
    rest = 8 * (2 * depth - 1)
    send(slot_out.at[pl.ds(0, rest)], slot_got.at[pl.ds(8, rest)], slot_sem, 0, to_core).wait()
    for c in range(2):
        high, low = halves(slot_got[pl.ds(c, LANES, stride=2), :])
        plane_out[pl.ds(c, 64, stride=2), :] = dot(adds[...], high) + dot(adds[...], low)

    for offset in NEAR:
        peer_x, peer_shell = plane_peer(offset)
        spot = NEAR.index((offset[0], -offset[1] % 4, offset[2]))
        send(
            plane_out.at[pl.ds(pl.multiple_of((peer_x * SHELLS + peer_shell) * 8, 8), 8)],
            plane_got.at[pl.ds(spot * 8, 8)],
            plane_sem,
            0,
            at(z * QUAD + peer_x * 2 + core, peer_shell),
        ).start()
    total = plane_out[pl.ds(pl.multiple_of((x_lo * SHELLS + shell) * 8, 8), 8), :]
    rest = 8 * len(NEAR)
    send(plane_out.at[pl.ds(0, rest)], plane_got, plane_sem, 0, to_core).wait()
    for i in range(len(NEAR)):
        total = total + plane_got[i * 8 : i * 8 + 8, :]
    out_ref[...] = total


NNZ = 4
NNZ_ROWS = NNZ


def shards(images, defocus, pose_bin, freq_sq, model_slice, interp_coef, block_index):
    depth = lax.axis_size("slab") // QUAD
    rows, _, width = images.shape
    vmem = pl.BlockSpec(memory_space=pltpu.VMEM)
    hbm = pl.BlockSpec(memory_space=pl.ANY)
    dma = pltpu.SemaphoreType.DMA
    out = pl.pallas_call(
        functools.partial(kernel, depth),
        out_shape=jax.ShapeDtypeStruct((8, LANES), F32),
        in_specs=[hbm] * 7,
        out_specs=vmem,
        scratch_shapes=[
            pltpu.VMEM((1, rows), jnp.int32),
            pltpu.VMEM((1, rows), BF16),
            pltpu.VMEM((width // LANES, LANES), F32),
            pltpu.VMEM((2, width), F32),
            pltpu.VMEM((NNZ, 16), jnp.int32),
            pltpu.VMEM((2 * rows, width), BF16),
            pltpu.VMEM(interp_coef.shape[1:], BF16),
            pltpu.VMEM((LANES, LANES), F32),
            pltpu.VMEM((LANES, 2 * LANES), BF16),
            pltpu.VMEM((2 * LANES, LANES), F32),
            [pltpu.VMEM((QUAD * depth, 2 * run * LANES), F32) for run in RUNS],
            [pltpu.VMEM((2 * depth, 2 * run * LANES), F32) for run in RUNS],
            [pltpu.VMEM((depth, 2 * run * LANES), F32) for run in RUNS],
            pltpu.VMEM((QUAD * depth, LANES), F32),
            pltpu.VMEM((2 * depth, LANES), F32),
            pltpu.VMEM((depth, LANES), F32),
            [pltpu.VMEM((depth, 2 * run, LANES), F32) for run in RUNS],
            [pltpu.VMEM((depth, 2 * run, LANES), BF16) for run in RUNS],
            [pltpu.VMEM((depth, 2 * run, LANES), BF16) for run in RUNS],
            pltpu.VMEM((depth, 1, LANES), F32),
            pltpu.VMEM((depth, 1, LANES), F32),
            pltpu.VMEM((QUAD * CAP, depth, LANES), F32),
            pltpu.VMEM((16, LANES), F32),
            pltpu.VMEM((32, LANES), F32),
            pltpu.VMEM((LANES, LANES), BF16),
            pltpu.VMEM((2 * depth, LANES), F32),
            pltpu.VMEM((depth, LANES), F32),
            pltpu.VMEM((64, LANES), BF16),
            pltpu.VMEM((LANES, 2 * LANES), F32),
            pltpu.VMEM((2 * LANES, LANES), F32),
            pltpu.VMEM((2 * LANES, LANES), F32),
            pltpu.VMEM((PLANE * 8, LANES), F32),
            pltpu.VMEM((len(NEAR) * 8, LANES), F32),
            pltpu.SemaphoreType.REGULAR,
            dma((5,)),
            dma((CHUNKS,)),
            dma,
            dma((2, CHUNKS + 2)),
            dma((2, CHUNKS + 1)),
            dma((2, CHUNKS)),
            dma((2,)),
            dma((2, 1)),
            dma((2, 1)),
        ],
        compiler_params=pltpu.CompilerParams(collective_id=0, has_side_effects=True, vmem_limit_bytes=20 << 20),
        name="cryo_grad",
    )(*(pltpu.with_memory_space_constraint(a, pltpu.HBM) for a in (
        pose_bin.reshape(1, rows),
        defocus.reshape(1, rows),
        freq_sq.reshape(width // LANES, LANES),
        model_slice[0],
        jnp.transpose(block_index[0]),
        images,
        interp_coef[0],
    )))
    return out.reshape(4, 2, LANES)


def solution(mesh):
    return jax.shard_map(
        shards,
        mesh=mesh,
        in_specs=(
            P("slab", None, "shell"),
            P("slab"),
            P("slab", None),
            P("shell"),
            P("slab", None, "shell"),
            P("slab", "shell", None, None, None),
            P("slab", "shell", None),
        ),
        out_specs=P(("slab", "shell"), None, None),
        check_vma=False,
    )
```

```python
import functools

import jax
import jax.numpy as jnp
from jax import lax
from jax.experimental import pallas as pl
from jax.experimental.pallas import tpu as pltpu
from jax.sharding import PartitionSpec as P

F32 = jnp.float32
BF16 = jnp.bfloat16
MESH = pl.DeviceIdType.MESH

QUAD = 4
SHELLS = 8
CAP = 6
LANES = 128
RUNS = (4, 4, 4, 4)
STARTS = tuple(sum(RUNS[:i]) for i in range(len(RUNS)))
CHUNKS = len(RUNS)
EARLY = (4, 12, 3, 13, 2, 14, 1, 15)
NEAR = [(dx, dy, dh) for dx in range(2) for dy in range(4) for dh in range(2)]
NEAR = sorted(NEAR, key=lambda d: -(min(d[1], 4 - d[1]) + abs(2 * d[2] - d[0])))[:-1]
PLANE = 16

INV_PI = 0.3183098861837907
PI_A, PI_B, PI_C = 3.140625, 9.67502593994140625e-4, 1.509957990978376e-7
S3, S5, S7, S9, S11 = -1 / 6, 1 / 120, -1 / 5040, 1 / 362880, -1 / 39916800


def folded(x):
    n = jnp.floor(x * INV_PI + 0.5)
    r = ((x - n * PI_A) - n * PI_B) - n * PI_C
    t = r * r
    return r * (1.0 + t * (S3 + t * (S5 + t * (S7 + t * (S9 + t * S11))))), n


def sine(x):
    s, n = folded(x)
    odd = n - 2.0 * jnp.floor(n * 0.5)
    return s * (1.0 - 2.0 * odd)


def dot(a, b):
    return jnp.dot(a, b, preferred_element_type=F32)


def halves(x):
    high = x.astype(BF16)
    return high, (x - high.astype(F32)).astype(BF16)


def iota(shape, dim):
    return lax.broadcasted_iota(jnp.int32, shape, dim)


def down(row):
    return jnp.broadcast_to(row, (LANES, LANES)).T


def kernel(
    depth,
    pose_hbm,
    focus_hbm,
    freq_hbm,
    model_hbm,
    index_hbm,
    images_ref,
    coef_ref,
    out_ref,
    pose_ref,
    focus_ref,
    freq_ref,
    model_ref,
    index_ref,
    img,
    coef,
    focus_col,
    pair_hot,
    spread,
    part,
    core_got,
    x_out,
    x_got,
    table,
    table_core,
    table_x,
    stage,
    z_out,
    z_got,
    note_out,
    note_got,
    column,
    power,
    resid,
    place,
    target,
    target_got,
    adds,
    terms,
    slot_stage,
    slot_out,
    slot_got,
    plane_out,
    plane_got,
    far_sem,
    small_sem,
    img_sem,
    coef_sem,
    core_sem,
    x_sem,
    z_sem,
    note_sem,
    slot_sem,
    plane_sem,
):
    slab = lax.axis_index("slab")
    shell = lax.axis_index("shell")
    z, quad = slab // QUAD, slab % QUAD
    x_lo, core = quad // 2, quad % 2
    core_peer = z * QUAD + x_lo * 2 + (1 - core)
    x_peer = z * QUAD + (1 - x_lo) * 2 + core
    y, x_hi = shell // 2, shell % 2

    def at(slab_id, shell_id):
        return {"slab": slab_id, "shell": shell_id}

    def z_peer(j):
        return lax.rem(z + j, depth)

    def plane_peer(offset):
        dx, dy, dh = offset
        return (x_lo + dx) % 2, (y + dy) % 4 * 2 + (x_hi + dh) % 2

    rows_ref = images_ref.reshape(2 * images_ref.shape[0], images_ref.shape[2])
    loads = [
        pltpu.make_async_copy(
            rows_ref.at[:, pl.ds(start * LANES, run * LANES)],
            img.at[:, pl.ds(start * LANES, run * LANES)],
            img_sem.at[ch],
        )
        for ch, (start, run) in enumerate(zip(STARTS, RUNS))
    ]
    smalls = [
        pltpu.make_async_copy(src, dst, small_sem.at[i])
        for i, (src, dst) in enumerate(
            (
                (pose_hbm, pose_ref),
                (focus_hbm, focus_ref),
                (freq_hbm, freq_ref),
                (index_hbm, index_ref),
                (model_hbm, model_ref),
            )
        )
    ]
    for load in smalls + loads:
        load.start()
    coef_load = pltpu.make_async_copy(coef_ref, coef, coef_sem)
    coef_load.start()

    barrier = pltpu.get_barrier_semaphore()

    far_first = sorted(range(1, depth), key=lambda j: -min(j, depth - j))
    reach = depth // 4
    close = [j for j in far_first if min(j, depth - j) <= reach]
    for j in close:
        pl.semaphore_signal(barrier, inc=1, device_id=at(z_peer(j) * QUAD + quad, shell), device_id_type=MESH)

    for offset in NEAR:
        peer_x, peer_shell = plane_peer(offset)
        pl.semaphore_signal(
            barrier, inc=1, device_id=at(z * QUAD + peer_x * 2 + core, peer_shell), device_id_type=MESH
        )
    pl.semaphore_signal(barrier, inc=1, device_id=at(core_peer, shell), device_id_type=MESH)

    smalls[0].wait()
    smalls[1].wait()
    pose = pose_ref[...].astype(F32)
    pose_col = down(pose)
    focus_col[...] = down(focus_ref[...].astype(F32))
    twice = (iota((LANES, 2 * LANES), 1) // 2 == iota((LANES, 2 * LANES), 0)).astype(F32).astype(BF16)
    pose_pair = dot(jnp.broadcast_to(pose, (8, LANES)).astype(BF16), twice)[0:1]
    wide = iota((LANES, 2 * LANES), 0)
    r64 = wide % 64
    bin64 = r64 % depth * QUAD + (r64 // depth) % 2 * 2 + r64 // (2 * depth)
    parity = iota((LANES, 2 * LANES), 1) % 2
    pair_hot[...] = (
        ((bin64.astype(F32) == pose_pair) & (parity == wide // 64)).astype(F32).astype(BF16)
    )

    half = 2 * depth
    other_rows = pl.multiple_of((1 - core) * half, half)
    my_rows = pl.multiple_of(core * half, half)
    other_x = pl.multiple_of(core * half + (1 - x_lo) * depth, depth)
    my_x = pl.multiple_of(core * half + x_lo * depth, depth)

    def send(src, dst, sems, i, device):
        return pltpu.make_async_remote_copy(
            src_ref=src,
            dst_ref=dst,
            send_sem=sems.at[0, i],
            recv_sem=sems.at[1, i],
            device_id=device,
            device_id_type=MESH,
        )

    to_core = at(core_peer, shell)
    to_x = at(x_peer, shell)

    def summed(ch):
        loads[ch].wait()

        @pl.loop(0, RUNS[ch])
        def _(q):
            k = STARTS[ch] + q
            contrast = sine(focus_col[...] * freq_ref[pl.ds(k, 1), :])
            spread[pl.ds(0, LANES, stride=2), :] = contrast
            spread[pl.ds(1, LANES, stride=2), :] = contrast
            picture = img[:, pl.ds(pl.multiple_of(k * LANES, LANES), LANES)].astype(F32)
            high, low = halves(spread[...] * picture)
            sums = dot(pair_hot[...], high) + dot(pair_hot[...], low)
            first = pl.multiple_of(q * LANES, LANES)
            second = pl.multiple_of(RUNS[ch] * LANES + first, LANES)
            part[ch][:, pl.ds(first, LANES)] = sums[0:64]
            part[ch][:, pl.ds(second, LANES)] = sums[64:128]

    core_sends = [
        send(part[ch].at[pl.ds(other_rows, half)], core_got[ch], core_sem, ch, to_core) for ch in range(CHUNKS)
    ]
    x_sends = [
        send(x_out[ch], x_got[ch], x_sem, ch, to_x) for ch in range(CHUNKS)
    ]

    def pass_on(ch):
        core_sends[ch].wait()
        part[ch][pl.ds(my_rows, half), :] += core_got[ch][...]
        x_out[ch][...] = part[ch][pl.ds(other_x, depth), :].astype(BF16)
        x_sends[ch].start()

    smalls[2].wait()
    summed(0)
    pl.semaphore_wait(barrier, len(close) + len(NEAR) + 1)
    core_sends[0].start()
    for j in (reach, depth - reach):
        pl.semaphore_signal(far_sem, inc=1, device_id=at(z_peer(j) * QUAD + quad, shell), device_id_type=MESH)

    same = (pose_col == pose) & (iota((LANES, LANES), 1) < iota((LANES, LANES), 0))
    rank = jnp.sum(same.astype(F32), axis=1, keepdims=True)
    lane = iota((LANES, LANES), 1)
    wanted = 64 + quad * CAP + rank.astype(jnp.int32)
    spots = jnp.where(lane == wanted, focus_col[...], 0.0).astype(BF16)
    row = iota((64, LANES), 0)
    bins = row % depth * QUAD + (row // depth) % 2 * 2 + row // (2 * depth)
    hot = (bins == pose_ref[...]).astype(F32).astype(BF16)
    table[...] = dot(hot, spots)
    smalls[3].wait()
    index = index_ref[...]
    k_of = (iota((16, LANES), 1) % 16 == iota((16, LANES), 0)).astype(F32).astype(BF16)
    mask = (iota((NNZ_ROWS, LANES), 1) // 16 == iota((NNZ_ROWS, LANES), 0)).astype(F32)
    slab_row = jnp.sum(dot((index // 32).astype(F32).astype(BF16), k_of) * mask, axis=0, keepdims=True)
    low_row = jnp.sum(dot((index % 32).astype(F32).astype(BF16), k_of) * mask, axis=0, keepdims=True)
    live = iota((1, LANES), 1) < 64
    slab_row = jnp.where(live, slab_row, -1.0)
    slab_col = down(slab_row)
    before = (slab_col == slab_row) & (iota((LANES, LANES), 0) < iota((LANES, LANES), 1))
    rank_row = jnp.sum(before.astype(F32), axis=0, keepdims=True).astype(jnp.int32)
    slab_int = slab_row.astype(jnp.int32)
    x_of = slab_int % QUAD // 2
    slot_row = jnp.where(live, slab_int % 2 * 64 + slab_int // QUAD * 4 + x_of * 2 + rank_row, -1)
    place[...] = (iota((LANES, LANES), 0) == slot_row).astype(F32).astype(BF16)
    block_row = (x_of * 32 + low_row.astype(jnp.int32) + 1).astype(F32)
    at_z = ((slot_row // 4 == iota((2 * depth, LANES), 0)) & live).astype(F32).astype(BF16)
    at_lane = jnp.where(slot_row % 4 == iota((LANES, LANES), 0), block_row, 0.0).astype(BF16)
    target[...] = lax.dot_general(at_z, at_lane, (((1,), (1,)), ((), ())), preferred_element_type=F32)

    other_targets = pl.multiple_of((1 - core) * depth, depth)
    my_targets = pl.multiple_of(core * depth, depth)
    table_send = send(table.at[pl.ds(other_rows, half)], table_core, core_sem, CHUNKS, to_core)
    target_send = send(target.at[pl.ds(other_targets, depth)], target_got, core_sem, CHUNKS + 1, to_core)
    table_send.start()
    target_send.start()

    table_x_send = send(table.at[pl.ds(other_x, depth)], table_x, x_sem, CHUNKS, to_x)
    for ch in range(1, CHUNKS):
        summed(ch)
        core_sends[ch].start()
        if ch == 1:
            pass_on(0)
            table_send.wait()
            table[pl.ds(my_rows, half), :] += table_core[...]
            table_x_send.start()
    for ch in range(1, CHUNKS):
        pass_on(ch)

    def along_z(out, got, i, j):
        peer = z_peer(j)
        return pltpu.make_async_remote_copy(
            src_ref=out.at[peer],
            dst_ref=got.at[depth - j],
            send_sem=i[0],
            recv_sem=i[1],
            device_id=at(peer * QUAD + quad, shell),
            device_id_type=MESH,
        )

    def all_of(out, got, i):
        return pltpu.make_async_remote_copy(
            src_ref=out.at[pl.ds(0, depth - 1)],
            dst_ref=got.at[pl.ds(1, depth - 1)],
            send_sem=i[0],
            recv_sem=i[1],
            device_id=at(z_peer(1) * QUAD + quad, shell),
            device_id_type=MESH,
        )

    note_sems = (note_sem.at[0], note_sem.at[1])

    def z_send(ch, to):
        for j in to:
            along_z(z_out[ch], z_got[ch], (z_sem.at[0, ch], z_sem.at[1, ch]), j).start()

    for ch in range(CHUNKS):
        x_sends[ch].wait()
        total = part[ch][pl.ds(my_x, depth), :] + x_got[ch][...].astype(F32)
        for b in range(2 * RUNS[ch]):
            stage[ch][:, b, :] = total[:, b * LANES : (b + 1) * LANES]
        z_out[ch][...] = stage[ch][...].astype(BF16)
        if ch > 0:
            z_send(ch, far_first)
            continue
        z_send(0, EARLY)
        pl.semaphore_wait(far_sem, 2)
        z_send(0, [j for j in far_first if j not in EARLY])
        table_x_send.wait()
        target_send.wait()
        own_table = table[pl.ds(my_x, depth), :] + table_x[...]
        note_out[:, 0, :] = own_table + target[pl.ds(my_targets, depth), :] + pltpu.roll(target_got[...], 4, 1)
        note_got[0] = note_out[z]

        for j in far_first:
            along_z(note_out, note_got, note_sems, j).start()
    all_of(note_out, note_got, note_sems).wait()
    values = note_got[:, 0, :]
    for i in range(QUAD * CAP):
        column[i] = jnp.broadcast_to(values[:, 64 + i : 65 + i], (depth, LANES))

    @pl.loop(0, sum(RUNS))
    def _(k):
        freq = freq_ref[pl.ds(k, 1), :]
        total = jnp.zeros((depth, LANES), F32)
        for i in range(QUAD * CAP):
            s, _ = folded(column[i] * freq)
            total = total + s * s
        power[pl.ds(k, 1), :] = jnp.sum(total, axis=0, keepdims=True)

    across = iota((LANES, LANES), 1)
    slot_of = (across // 64 * 4 + across % 4 == iota((LANES, LANES), 0)).astype(F32).astype(BF16)
    from_z = (iota((depth, LANES), 1) % 64 // 4 == iota((depth, LANES), 0)).astype(F32)
    to_block = jnp.sum(dot(values.astype(BF16), slot_of) * from_z, axis=0, keepdims=True)
    adds[...] = (to_block == (iota((64, LANES), 0) + 1).astype(F32)).astype(F32).astype(BF16)
    terms[...] = jnp.zeros_like(terms)
    coef_load.wait()
    smalls[4].wait()

    for ch in range(CHUNKS):
        all_of(z_out[ch], z_got[ch], (z_sem.at[0, ch], z_sem.at[1, ch])).wait()
        numerator = stage[ch][z]
        for j in range(1, depth):
            numerator = numerator + z_got[ch][j].astype(F32)
        for c in range(2):
            for q in range(RUNS[ch]):
                k = STARTS[ch] + q
                model = model_ref[c : c + 1, k * LANES : (k + 1) * LANES]
                resid[c * 16 + k : c * 16 + k + 1, :] = (
                    power[k : k + 1, :] * model - numerator[c * RUNS[ch] + q : c * RUNS[ch] + q + 1, :]
                ) * (1.0 / 128)
        for q in range(RUNS[ch]):
            k = STARTS[ch] + q
            left = jnp.concatenate([resid[k : k + 1, :], resid[16 + k : 17 + k, :]], axis=0).astype(BF16)
            for j in range(NNZ):
                term = dot(left, coef[k, j])
                t = j * 16 + k
                terms[t : t + 1, 0:LANES] = term[0:1]
                terms[t : t + 1, LANES : 2 * LANES] = term[1:2]

    high, low = halves(terms[...])
    slots = dot(place[...], high) + dot(place[...], low)
    slot_stage[pl.ds(0, LANES, stride=2), :] = slots[:, 0:LANES]
    slot_stage[pl.ds(1, LANES, stride=2), :] = slots[:, LANES : 2 * LANES]
    slot_out[...] = slot_stage[...].reshape(2 * depth, 8, LANES).astype(BF16)
    for j in far_first + [0]:
        for other in range(2):
            if j or other:
                side = 1 - core if other else core
                peer = z_peer(j)
                send(
                    slot_out.at[side * depth + peer],
                    slot_got.at[other * depth + (depth - j) % depth],
                    slot_sem,
                    0,
                    at(peer * QUAD + x_lo * 2 + side, shell),
                ).start()
    slot_got[0] = slot_out[core * depth + z]
    rest = 2 * depth - 1
    send(slot_out.at[pl.ds(0, rest)], slot_got.at[pl.ds(1, rest)], slot_sem, 0, to_core).wait()
    slot_stage[...] = slot_got[...].astype(F32).reshape(2 * LANES, LANES)
    for c in range(2):
        plane_out[pl.ds(c, 64, stride=2), :] = dot(adds[...], slot_stage[pl.ds(c, LANES, stride=2), :].astype(BF16))

    for offset in NEAR:
        peer_x, peer_shell = plane_peer(offset)
        spot = NEAR.index((offset[0], -offset[1] % 4, offset[2]))
        send(
            plane_out.at[pl.ds(pl.multiple_of((peer_x * SHELLS + peer_shell) * 8, 8), 8)],
            plane_got.at[pl.ds(spot * 8, 8)],
            plane_sem,
            0,
            at(z * QUAD + peer_x * 2 + core, peer_shell),
        ).start()
    total = plane_out[pl.ds(pl.multiple_of((x_lo * SHELLS + shell) * 8, 8), 8), :]
    rest = 8 * len(NEAR)
    send(plane_out.at[pl.ds(0, rest)], plane_got, plane_sem, 0, to_core).wait()
    for i in range(len(NEAR)):
        total = total + plane_got[i * 8 : i * 8 + 8, :]
    out_ref[...] = total


NNZ = 4
NNZ_ROWS = NNZ


def shards(images, defocus, pose_bin, freq_sq, model_slice, interp_coef, block_index):
    depth = lax.axis_size("slab") // QUAD
    rows, _, width = images.shape
    vmem = pl.BlockSpec(memory_space=pltpu.VMEM)
    hbm = pl.BlockSpec(memory_space=pl.ANY)
    dma = pltpu.SemaphoreType.DMA
    out = pl.pallas_call(
        functools.partial(kernel, depth),
        out_shape=jax.ShapeDtypeStruct((8, LANES), F32),
        in_specs=[hbm] * 7,
        out_specs=vmem,
        scratch_shapes=[
            pltpu.VMEM((1, rows), jnp.int32),
            pltpu.VMEM((1, rows), BF16),
            pltpu.VMEM((width // LANES, LANES), F32),
            pltpu.VMEM((2, width), F32),
            pltpu.VMEM((NNZ, 16), jnp.int32),
            pltpu.VMEM((2 * rows, width), BF16),
            pltpu.VMEM(interp_coef.shape[1:], BF16),
            pltpu.VMEM((LANES, LANES), F32),
            pltpu.VMEM((LANES, 2 * LANES), BF16),
            pltpu.VMEM((2 * LANES, LANES), F32),
            [pltpu.VMEM((QUAD * depth, 2 * run * LANES), F32) for run in RUNS],
            [pltpu.VMEM((2 * depth, 2 * run * LANES), F32) for run in RUNS],
            [pltpu.VMEM((depth, 2 * run * LANES), BF16) for run in RUNS],
            [pltpu.VMEM((depth, 2 * run * LANES), BF16) for run in RUNS],
            pltpu.VMEM((QUAD * depth, LANES), F32),
            pltpu.VMEM((2 * depth, LANES), F32),
            pltpu.VMEM((depth, LANES), F32),
            [pltpu.VMEM((depth, 2 * run, LANES), F32) for run in RUNS],
            [pltpu.VMEM((depth, 2 * run, LANES), BF16) for run in RUNS],
            [pltpu.VMEM((depth, 2 * run, LANES), BF16) for run in RUNS],
            pltpu.VMEM((depth, 1, LANES), F32),
            pltpu.VMEM((depth, 1, LANES), F32),
            pltpu.VMEM((QUAD * CAP, depth, LANES), F32),
            pltpu.VMEM((16, LANES), F32),
            pltpu.VMEM((32, LANES), F32),
            pltpu.VMEM((LANES, LANES), BF16),
            pltpu.VMEM((2 * depth, LANES), F32),
            pltpu.VMEM((depth, LANES), F32),
            pltpu.VMEM((64, LANES), BF16),
            pltpu.VMEM((LANES, 2 * LANES), F32),
            pltpu.VMEM((2 * LANES, LANES), F32),
            pltpu.VMEM((2 * depth, 8, LANES), BF16),
            pltpu.VMEM((2 * depth, 8, LANES), BF16),
            pltpu.VMEM((PLANE * 8, LANES), F32),
            pltpu.VMEM((len(NEAR) * 8, LANES), F32),
            pltpu.SemaphoreType.REGULAR,
            dma((5,)),
            dma((CHUNKS,)),
            dma,
            dma((2, CHUNKS + 2)),
            dma((2, CHUNKS + 1)),
            dma((2, CHUNKS)),
            dma((2,)),
            dma((2, 1)),
            dma((2, 1)),
        ],
        compiler_params=pltpu.CompilerParams(collective_id=0, has_side_effects=True, vmem_limit_bytes=20 << 20),
        name="cryo_grad",
    )(*(pltpu.with_memory_space_constraint(a, pltpu.HBM) for a in (
        pose_bin.reshape(1, rows),
        defocus.reshape(1, rows),
        freq_sq.reshape(width // LANES, LANES),
        model_slice[0],
        jnp.transpose(block_index[0]),
        images,
        interp_coef[0],
    )))
    return out.reshape(4, 2, LANES)


def solution(mesh):
    return jax.shard_map(
        shards,
        mesh=mesh,
        in_specs=(
            P("slab", None, "shell"),
            P("slab"),
            P("slab", None),
            P("shell"),
            P("slab", None, "shell"),
            P("slab", "shell", None, None, None),
            P("slab", "shell", None),
        ),
        out_specs=P(("slab", "shell"), None, None),
        check_vma=False,
    )
```

```python
import functools

import jax
import jax.numpy as jnp
from jax import lax
from jax.experimental import pallas as pl
from jax.experimental.pallas import tpu as pltpu
from jax.sharding import PartitionSpec as P

F32 = jnp.float32
BF16 = jnp.bfloat16
MESH = pl.DeviceIdType.MESH

QUAD = 4
SHELLS = 8
CAP = 6
LANES = 128
RUNS = (4, 4, 4, 4)
STARTS = tuple(sum(RUNS[:i]) for i in range(len(RUNS)))
CHUNKS = len(RUNS)
EARLY = (4, 12, 3, 13, 2, 14, 1, 15)
NEAR = [(dx, dy, dh) for dx in range(2) for dy in range(4) for dh in range(2)]
NEAR = sorted(NEAR, key=lambda d: -(min(d[1], 4 - d[1]) + abs(2 * d[2] - d[0])))[:-1]
PLANE = 16

INV_PI = 0.3183098861837907
PI_A, PI_B, PI_C = 3.140625, 9.67502593994140625e-4, 1.509957990978376e-7
S3, S5, S7, S9, S11 = -1 / 6, 1 / 120, -1 / 5040, 1 / 362880, -1 / 39916800


def folded(x):
    n = jnp.floor(x * INV_PI + 0.5)
    r = ((x - n * PI_A) - n * PI_B) - n * PI_C
    t = r * r
    return r * (1.0 + t * (S3 + t * (S5 + t * (S7 + t * (S9 + t * S11))))), n


def sine(x):
    s, n = folded(x)
    odd = n - 2.0 * jnp.floor(n * 0.5)
    return s * (1.0 - 2.0 * odd)


def dot(a, b):
    return jnp.dot(a, b, preferred_element_type=F32)


def halves(x):
    high = x.astype(BF16)
    return high, (x - high.astype(F32)).astype(BF16)


def iota(shape, dim):
    return lax.broadcasted_iota(jnp.int32, shape, dim)


def down(row):
    return jnp.broadcast_to(row, (LANES, LANES)).T


def kernel(
    depth,
    pose_hbm,
    focus_hbm,
    freq_hbm,
    model_hbm,
    index_hbm,
    images_ref,
    coef_ref,
    out_ref,
    pose_ref,
    focus_ref,
    freq_ref,
    model_ref,
    index_ref,
    img,
    coef,
    focus_col,
    pair_hot,
    spread,
    part,
    core_got,
    x_out,
    x_got,
    table,
    table_core,
    table_x,
    stage,
    z_out,
    z_got,
    note_out,
    note_got,
    column,
    power,
    resid,
    place,
    target,
    target_got,
    adds,
    terms,
    slot_stage,
    slot_out,
    slot_got,
    plane_out,
    plane_got,
    far_sem,
    small_sem,
    img_sem,
    coef_sem,
    core_sem,
    x_sem,
    z_sem,
    note_sem,
    slot_sem,
    plane_sem,
):
    slab = lax.axis_index("slab")
    shell = lax.axis_index("shell")
    z, quad = slab // QUAD, slab % QUAD
    x_lo, core = quad // 2, quad % 2
    core_peer = z * QUAD + x_lo * 2 + (1 - core)
    x_peer = z * QUAD + (1 - x_lo) * 2 + core
    y, x_hi = shell // 2, shell % 2

    def at(slab_id, shell_id):
        return {"slab": slab_id, "shell": shell_id}

    def z_peer(j):
        return lax.rem(z + j, depth)

    def plane_peer(offset):
        dx, dy, dh = offset
        return (x_lo + dx) % 2, (y + dy) % 4 * 2 + (x_hi + dh) % 2

    rows_ref = images_ref.reshape(2 * images_ref.shape[0], images_ref.shape[2])
    loads = [
        pltpu.make_async_copy(
            rows_ref.at[:, pl.ds(start * LANES, run * LANES)],
            img.at[:, pl.ds(start * LANES, run * LANES)],
            img_sem.at[ch],
        )
        for ch, (start, run) in enumerate(zip(STARTS, RUNS))
    ]
    smalls = [
        pltpu.make_async_copy(src, dst, small_sem.at[i])
        for i, (src, dst) in enumerate(
            (
                (pose_hbm, pose_ref),
                (focus_hbm, focus_ref),
                (freq_hbm, freq_ref),
                (index_hbm, index_ref),
                (model_hbm, model_ref),
            )
        )
    ]
    for load in smalls + loads:
        load.start()
    coef_load = pltpu.make_async_copy(coef_ref, coef, coef_sem)
    coef_load.start()

    barrier = pltpu.get_barrier_semaphore()

    far_first = sorted(range(1, depth), key=lambda j: -min(j, depth - j))
    reach = depth // 4
    close = [j for j in far_first if min(j, depth - j) <= reach]
    for j in close:
        pl.semaphore_signal(barrier, inc=1, device_id=at(z_peer(j) * QUAD + quad, shell), device_id_type=MESH)

    for offset in NEAR:
        peer_x, peer_shell = plane_peer(offset)
        pl.semaphore_signal(
            barrier, inc=1, device_id=at(z * QUAD + peer_x * 2 + core, peer_shell), device_id_type=MESH
        )
    pl.semaphore_signal(barrier, inc=1, device_id=at(core_peer, shell), device_id_type=MESH)

    smalls[0].wait()
    smalls[1].wait()
    pose = pose_ref[...].astype(F32)
    pose_col = down(pose)
    focus_col[...] = down(focus_ref[...].astype(F32))
    twice = (iota((LANES, 2 * LANES), 1) // 2 == iota((LANES, 2 * LANES), 0)).astype(F32).astype(BF16)
    pose_pair = dot(jnp.broadcast_to(pose, (8, LANES)).astype(BF16), twice)[0:1]
    wide = iota((LANES, 2 * LANES), 0)
    r64 = wide % 64
    bin64 = r64 % depth * QUAD + (r64 // depth) % 2 * 2 + r64 // (2 * depth)
    parity = iota((LANES, 2 * LANES), 1) % 2
    pair_hot[...] = (
        ((bin64.astype(F32) == pose_pair) & (parity == wide // 64)).astype(F32).astype(BF16)
    )

    half = 2 * depth
    other_rows = pl.multiple_of((1 - core) * half, half)
    my_rows = pl.multiple_of(core * half, half)
    other_x = pl.multiple_of(core * half + (1 - x_lo) * depth, depth)
    my_x = pl.multiple_of(core * half + x_lo * depth, depth)

    def send(src, dst, sems, i, device):
        return pltpu.make_async_remote_copy(
            src_ref=src,
            dst_ref=dst,
            send_sem=sems.at[0, i],
            recv_sem=sems.at[1, i],
            device_id=device,
            device_id_type=MESH,
        )

    to_core = at(core_peer, shell)
    to_x = at(x_peer, shell)

    def summed(ch):
        loads[ch].wait()

        for q in range(RUNS[ch]):
            k = STARTS[ch] + q
            contrast = sine(focus_col[...] * freq_ref[k : k + 1, :])
            spread[q, pl.ds(0, LANES, stride=2), :] = contrast
            spread[q, pl.ds(1, LANES, stride=2), :] = contrast
            picture = img[:, k * LANES : (k + 1) * LANES].astype(F32)
            high, low = halves(spread[q] * picture)
            sums = dot(pair_hot[...], high) + dot(pair_hot[...], low)
            second = RUNS[ch] + q
            part[ch][:, q * LANES : (q + 1) * LANES] = sums[0:64]
            part[ch][:, second * LANES : (second + 1) * LANES] = sums[64:128]

    core_sends = [
        send(part[ch].at[pl.ds(other_rows, half)], core_got[ch], core_sem, ch, to_core) for ch in range(CHUNKS)
    ]
    x_sends = [
        send(x_out[ch], x_got[ch], x_sem, ch, to_x) for ch in range(CHUNKS)
    ]

    def pass_on(ch):
        core_sends[ch].wait()
        part[ch][pl.ds(my_rows, half), :] += core_got[ch][...]
        x_out[ch][...] = part[ch][pl.ds(other_x, depth), :].astype(BF16)
        x_sends[ch].start()

    smalls[2].wait()
    summed(0)
    pl.semaphore_wait(barrier, len(close) + len(NEAR) + 1)
    core_sends[0].start()
    for j in (reach, depth - reach):
        pl.semaphore_signal(far_sem, inc=1, device_id=at(z_peer(j) * QUAD + quad, shell), device_id_type=MESH)

    same = (pose_col == pose) & (iota((LANES, LANES), 1) < iota((LANES, LANES), 0))
    rank = jnp.sum(same.astype(F32), axis=1, keepdims=True)
    lane = iota((LANES, LANES), 1)
    wanted = 64 + quad * CAP + rank.astype(jnp.int32)
    spots = jnp.where(lane == wanted, focus_col[...], 0.0).astype(BF16)
    row = iota((64, LANES), 0)
    bins = row % depth * QUAD + (row // depth) % 2 * 2 + row // (2 * depth)
    hot = (bins == pose_ref[...]).astype(F32).astype(BF16)
    table[...] = dot(hot, spots)
    smalls[3].wait()
    index = index_ref[...]
    k_of = (iota((16, LANES), 1) % 16 == iota((16, LANES), 0)).astype(F32).astype(BF16)
    mask = (iota((NNZ_ROWS, LANES), 1) // 16 == iota((NNZ_ROWS, LANES), 0)).astype(F32)
    slab_row = jnp.sum(dot((index // 32).astype(F32).astype(BF16), k_of) * mask, axis=0, keepdims=True)
    low_row = jnp.sum(dot((index % 32).astype(F32).astype(BF16), k_of) * mask, axis=0, keepdims=True)
    live = iota((1, LANES), 1) < 64
    slab_row = jnp.where(live, slab_row, -1.0)
    slab_col = down(slab_row)
    before = (slab_col == slab_row) & (iota((LANES, LANES), 0) < iota((LANES, LANES), 1))
    rank_row = jnp.sum(before.astype(F32), axis=0, keepdims=True).astype(jnp.int32)
    slab_int = slab_row.astype(jnp.int32)
    x_of = slab_int % QUAD // 2
    slot_row = jnp.where(live, slab_int % 2 * 64 + slab_int // QUAD * 4 + x_of * 2 + rank_row, -1)
    place[...] = (iota((LANES, LANES), 0) == slot_row).astype(F32).astype(BF16)
    block_row = (x_of * 32 + low_row.astype(jnp.int32) + 1).astype(F32)
    at_z = ((slot_row // 4 == iota((2 * depth, LANES), 0)) & live).astype(F32).astype(BF16)
    at_lane = jnp.where(slot_row % 4 == iota((LANES, LANES), 0), block_row, 0.0).astype(BF16)
    target[...] = lax.dot_general(at_z, at_lane, (((1,), (1,)), ((), ())), preferred_element_type=F32)

    other_targets = pl.multiple_of((1 - core) * depth, depth)
    my_targets = pl.multiple_of(core * depth, depth)
    table_send = send(table.at[pl.ds(other_rows, half)], table_core, core_sem, CHUNKS, to_core)
    target_send = send(target.at[pl.ds(other_targets, depth)], target_got, core_sem, CHUNKS + 1, to_core)
    table_send.start()
    target_send.start()

    table_x_send = send(table.at[pl.ds(other_x, depth)], table_x, x_sem, CHUNKS, to_x)
    for ch in range(1, CHUNKS):
        summed(ch)
        core_sends[ch].start()
        if ch == 2:
            pass_on(1)
        if ch == 1:
            pass_on(0)
            table_send.wait()
            table[pl.ds(my_rows, half), :] += table_core[...]
            table_x_send.start()
    for ch in range(2, CHUNKS):
        pass_on(ch)

    def along_z(out, got, i, j):
        peer = z_peer(j)
        return pltpu.make_async_remote_copy(
            src_ref=out.at[peer],
            dst_ref=got.at[depth - j],
            send_sem=i[0],
            recv_sem=i[1],
            device_id=at(peer * QUAD + quad, shell),
            device_id_type=MESH,
        )

    def all_of(out, got, i):
        return pltpu.make_async_remote_copy(
            src_ref=out.at[pl.ds(0, depth - 1)],
            dst_ref=got.at[pl.ds(1, depth - 1)],
            send_sem=i[0],
            recv_sem=i[1],
            device_id=at(z_peer(1) * QUAD + quad, shell),
            device_id_type=MESH,
        )

    note_sems = (note_sem.at[0], note_sem.at[1])

    def z_send(ch, to):
        for j in to:
            along_z(z_out[ch], z_got[ch], (z_sem.at[0, ch], z_sem.at[1, ch]), j).start()

    for ch in range(CHUNKS):
        x_sends[ch].wait()
        total = part[ch][pl.ds(my_x, depth), :] + x_got[ch][...].astype(F32)
        for b in range(2 * RUNS[ch]):
            stage[ch][:, b, :] = total[:, b * LANES : (b + 1) * LANES]
        z_out[ch][...] = stage[ch][...].astype(BF16)
        if ch > 0:
            z_send(ch, far_first)
            continue
        z_send(0, EARLY)
        pl.semaphore_wait(far_sem, 2)
        z_send(0, [j for j in far_first if j not in EARLY])
        table_x_send.wait()
        target_send.wait()
        own_table = table[pl.ds(my_x, depth), :] + table_x[...]
        note_out[:, 0, :] = own_table + target[pl.ds(my_targets, depth), :] + pltpu.roll(target_got[...], 4, 1)
        note_got[0] = note_out[z]

        for j in far_first:
            along_z(note_out, note_got, note_sems, j).start()
    all_of(note_out, note_got, note_sems).wait()
    values = note_got[:, 0, :]
    for i in range(QUAD * CAP):
        column[i] = jnp.broadcast_to(values[:, 64 + i : 65 + i], (depth, LANES))

    @pl.loop(0, sum(RUNS))
    def _(k):
        freq = freq_ref[pl.ds(k, 1), :]
        total = jnp.zeros((depth, LANES), F32)
        for i in range(QUAD * CAP):
            s, _ = folded(column[i] * freq)
            total = total + s * s
        power[pl.ds(k, 1), :] = jnp.sum(total, axis=0, keepdims=True)

    across = iota((LANES, LANES), 1)
    slot_of = (across // 64 * 4 + across % 4 == iota((LANES, LANES), 0)).astype(F32).astype(BF16)
    from_z = (iota((depth, LANES), 1) % 64 // 4 == iota((depth, LANES), 0)).astype(F32)
    to_block = jnp.sum(dot(values.astype(BF16), slot_of) * from_z, axis=0, keepdims=True)
    adds[...] = (to_block == (iota((64, LANES), 0) + 1).astype(F32)).astype(F32).astype(BF16)
    terms[...] = jnp.zeros_like(terms)
    coef_load.wait()
    smalls[4].wait()

    for ch in range(CHUNKS):
        all_of(z_out[ch], z_got[ch], (z_sem.at[0, ch], z_sem.at[1, ch])).wait()
        numerator = stage[ch][z]
        for j in range(1, depth):
            numerator = numerator + z_got[ch][j].astype(F32)
        for c in range(2):
            for q in range(RUNS[ch]):
                k = STARTS[ch] + q
                model = model_ref[c : c + 1, k * LANES : (k + 1) * LANES]
                resid[c * 16 + k : c * 16 + k + 1, :] = (
                    power[k : k + 1, :] * model - numerator[c * RUNS[ch] + q : c * RUNS[ch] + q + 1, :]
                ) * (1.0 / 128)
        for q in range(RUNS[ch]):
            k = STARTS[ch] + q
            left = jnp.concatenate([resid[k : k + 1, :], resid[16 + k : 17 + k, :]], axis=0).astype(BF16)
            for j in range(NNZ):
                term = dot(left, coef[k, j])
                t = j * 16 + k
                terms[t : t + 1, 0:LANES] = term[0:1]
                terms[t : t + 1, LANES : 2 * LANES] = term[1:2]

    high, low = halves(terms[...])
    slots = dot(place[...], high) + dot(place[...], low)
    slot_stage[pl.ds(0, LANES, stride=2), :] = slots[:, 0:LANES]
    slot_stage[pl.ds(1, LANES, stride=2), :] = slots[:, LANES : 2 * LANES]
    slot_out[...] = slot_stage[...].reshape(2 * depth, 8, LANES).astype(BF16)
    for j in far_first + [0]:
        for other in range(2):
            if j or other:
                side = 1 - core if other else core
                peer = z_peer(j)
                send(
                    slot_out.at[side * depth + peer],
                    slot_got.at[other * depth + (depth - j) % depth],
                    slot_sem,
                    0,
                    at(peer * QUAD + x_lo * 2 + side, shell),
                ).start()
    slot_got[0] = slot_out[core * depth + z]
    rest = 2 * depth - 1
    send(slot_out.at[pl.ds(0, rest)], slot_got.at[pl.ds(1, rest)], slot_sem, 0, to_core).wait()
    slot_stage[...] = slot_got[...].astype(F32).reshape(2 * LANES, LANES)
    for c in range(2):
        plane_out[pl.ds(c, 64, stride=2), :] = dot(adds[...], slot_stage[pl.ds(c, LANES, stride=2), :].astype(BF16))

    for offset in NEAR:
        peer_x, peer_shell = plane_peer(offset)
        spot = NEAR.index((offset[0], -offset[1] % 4, offset[2]))
        send(
            plane_out.at[pl.ds(pl.multiple_of((peer_x * SHELLS + peer_shell) * 8, 8), 8)],
            plane_got.at[pl.ds(spot * 8, 8)],
            plane_sem,
            0,
            at(z * QUAD + peer_x * 2 + core, peer_shell),
        ).start()
    total = plane_out[pl.ds(pl.multiple_of((x_lo * SHELLS + shell) * 8, 8), 8), :]
    rest = 8 * len(NEAR)
    send(plane_out.at[pl.ds(0, rest)], plane_got, plane_sem, 0, to_core).wait()
    for i in range(len(NEAR)):
        total = total + plane_got[i * 8 : i * 8 + 8, :]
    out_ref[...] = total


NNZ = 4
NNZ_ROWS = NNZ


def shards(images, defocus, pose_bin, freq_sq, model_slice, interp_coef, block_index):
    depth = lax.axis_size("slab") // QUAD
    rows, _, width = images.shape
    vmem = pl.BlockSpec(memory_space=pltpu.VMEM)
    hbm = pl.BlockSpec(memory_space=pl.ANY)
    dma = pltpu.SemaphoreType.DMA
    out = pl.pallas_call(
        functools.partial(kernel, depth),
        out_shape=jax.ShapeDtypeStruct((8, LANES), F32),
        in_specs=[hbm] * 7,
        out_specs=vmem,
        scratch_shapes=[
            pltpu.VMEM((1, rows), jnp.int32),
            pltpu.VMEM((1, rows), BF16),
            pltpu.VMEM((width // LANES, LANES), F32),
            pltpu.VMEM((2, width), F32),
            pltpu.VMEM((NNZ, 16), jnp.int32),
            pltpu.VMEM((2 * rows, width), BF16),
            pltpu.VMEM(interp_coef.shape[1:], BF16),
            pltpu.VMEM((LANES, LANES), F32),
            pltpu.VMEM((LANES, 2 * LANES), BF16),
            pltpu.VMEM((max(RUNS), 2 * LANES, LANES), F32),
            [pltpu.VMEM((QUAD * depth, 2 * run * LANES), F32) for run in RUNS],
            [pltpu.VMEM((2 * depth, 2 * run * LANES), F32) for run in RUNS],
            [pltpu.VMEM((depth, 2 * run * LANES), BF16) for run in RUNS],
            [pltpu.VMEM((depth, 2 * run * LANES), BF16) for run in RUNS],
            pltpu.VMEM((QUAD * depth, LANES), F32),
            pltpu.VMEM((2 * depth, LANES), F32),
            pltpu.VMEM((depth, LANES), F32),
            [pltpu.VMEM((depth, 2 * run, LANES), F32) for run in RUNS],
            [pltpu.VMEM((depth, 2 * run, LANES), BF16) for run in RUNS],
            [pltpu.VMEM((depth, 2 * run, LANES), BF16) for run in RUNS],
            pltpu.VMEM((depth, 1, LANES), F32),
            pltpu.VMEM((depth, 1, LANES), F32),
            pltpu.VMEM((QUAD * CAP, depth, LANES), F32),
            pltpu.VMEM((16, LANES), F32),
            pltpu.VMEM((32, LANES), F32),
            pltpu.VMEM((LANES, LANES), BF16),
            pltpu.VMEM((2 * depth, LANES), F32),
            pltpu.VMEM((depth, LANES), F32),
            pltpu.VMEM((64, LANES), BF16),
            pltpu.VMEM((LANES, 2 * LANES), F32),
            pltpu.VMEM((2 * LANES, LANES), F32),
            pltpu.VMEM((2 * depth, 8, LANES), BF16),
            pltpu.VMEM((2 * depth, 8, LANES), BF16),
            pltpu.VMEM((PLANE * 8, LANES), F32),
            pltpu.VMEM((len(NEAR) * 8, LANES), F32),
            pltpu.SemaphoreType.REGULAR,
            dma((5,)),
            dma((CHUNKS,)),
            dma,
            dma((2, CHUNKS + 2)),
            dma((2, CHUNKS + 1)),
            dma((2, CHUNKS)),
            dma((2,)),
            dma((2, 1)),
            dma((2, 1)),
        ],
        compiler_params=pltpu.CompilerParams(collective_id=0, has_side_effects=True, vmem_limit_bytes=20 << 20),
        name="cryo_grad",
    )(*(pltpu.with_memory_space_constraint(a, pltpu.HBM) for a in (
        pose_bin.reshape(1, rows),
        defocus.reshape(1, rows),
        freq_sq.reshape(width // LANES, LANES),
        model_slice[0],
        jnp.transpose(block_index[0]),
        images,
        interp_coef[0],
    )))
    return out.reshape(4, 2, LANES)


def solution(mesh):
    return jax.shard_map(
        shards,
        mesh=mesh,
        in_specs=(
            P("slab", None, "shell"),
            P("slab"),
            P("slab", None),
            P("shell"),
            P("slab", None, "shell"),
            P("slab", "shell", None, None, None),
            P("slab", "shell", None),
        ),
        out_specs=P(("slab", "shell"), None, None),
        check_vma=False,
    )
```
